32 devices in a mesh: cluster: 16 (over z, y, x), ens: 2 (over core).
Axes of the slice: x: 2, y: 2, z: 4, core: 2. Of those that a mesh axis runs over, the one named last changes fastest.
Arguments:
- log_rate: float32 [16, 16384], P('ens', 'cluster'), may hold values from -1 to 0.5
- state: float32 [16, 16384], P('ens', 'cluster'), may hold values from -1 to 1
- rate_coef: float32 [16, 16384], P('ens', 'cluster'), may hold values from 0.5 to 2
- state_coef: float32 [16, 16384], P('ens', 'cluster'), may hold values from 0.5 to 2
- near_weight: bfloat16 [3, 16384, 1024], P(None, 'cluster', 'ens'), may hold values from -0.21582031 to 0.21582031
- col_basis: bfloat16 [64, 16384], P(None, 'cluster'), may hold values from -0.1875 to 0.1875
- coupling: float32 [1024, 1024], P('cluster'), may hold values from -0.1875 to 0.1875
- cluster_row_factors: float32 [64, 16384], P(None, 'cluster'), may hold values from -2.25 to 2.25
- ranks: int32 [16], P('cluster'), may hold values from 16 to 64, as said below
Outputs:
- log_rate_next: float32 [16, 16384], P('ens', 'cluster')
- state_next: float32 [16, 16384], P('ens', 'cluster')
The draws below stay inside these ranges and needn't reach their ends.
Inputs may be any that keep to these rules, and one draw needn't show every extreme that they name: `ranks`: each cluster's rank lies in 16 to 64; some cluster has rank 64.
All inputs are finite; a program needn't handle non-finite values.
Results may differ from the reference program's by a relative error of at most 0.0017.
Values may be sent and summed in bfloat16 or wider, within the bound.
A program may use at most 64 MiB of HBM per device.

```python
import math
import jax
import jax.numpy as jnp
from jax import lax

CLUSTER_ROWS = 1024
LARGEST_RANK = 64
CLUSTER_TOTAL = 16
TRIS = 16384
MEMBERS = 16


def draw_ranks(key, part):
    first, second = jax.random.split(key)
    values = jax.random.randint(first, (CLUSTER_TOTAL,), LARGEST_RANK // 4, LARGEST_RANK + 1)
    widest = jax.random.randint(second, (), 0, CLUSTER_TOTAL)
    return values.at[widest].set(LARGEST_RANK).astype(jnp.int32)


def steps_of(rng, dims, cuts, least, top_value):
    def one(axis_at, parts):
        draws = jax.random.uniform(jax.random.fold_in(jax.random.fold_in(rng, 6), axis_at), (parts,), jnp.float32, least / len(cuts), top_value / len(cuts))
        return jnp.repeat(jnp.exp(draws), dims[axis_at] // parts).reshape((-1,) + (1,) * (len(dims) - axis_at - 1))

    gain = one(*cuts[0])
    for cut in cuts[1:]:
        gain = gain * one(*cut)
    return gain


def scatter_about(own_key, extent, deviation, bound, cuts=(), kind=jnp.bfloat16):
    gain = steps_of(own_key, extent, cuts, -0.22, 0.18) if cuts else 1.0
    array = jax.random.normal(own_key, extent, jnp.float32) * deviation * gain
    return jnp.minimum(jnp.maximum(array, -bound), bound).astype(kind)


def setup_inputs(seed: int = 0) -> dict:
    splits = jax.random.split(jax.random.key(seed), 10)
    return {
        "log_rate": jnp.clip(-1.0 + 1.5 * jax.random.uniform(splits[0], (MEMBERS, TRIS), jnp.float32) ** steps_of(splits[0], (MEMBERS, TRIS), ((0, 2), (1, 16)), -0.2, 0.2), -1.0, 0.5),
        "state": jnp.clip(jax.random.uniform(splits[1], (MEMBERS, TRIS), jnp.float32, -1.0, 1.0) * steps_of(splits[1], (MEMBERS, TRIS), ((0, 2), (1, 16)), -0.4, 0.0), -1.0, 1.0),
        "rate_coef": jnp.clip(jnp.exp(math.log(2.0) - 1.3862944 * jax.random.uniform(splits[2], (MEMBERS, TRIS), jnp.float32) ** steps_of(splits[2], (MEMBERS, TRIS), ((0, 2), (1, 16)), -0.2, 0.2)), 0.5, 2.0),
        "state_coef": jnp.clip(jnp.exp(math.log(2.0) - 1.3862944 * jax.random.uniform(splits[3], (MEMBERS, TRIS), jnp.float32) ** steps_of(splits[3], (MEMBERS, TRIS), ((0, 2), (1, 16)), -0.2, 0.2)), 0.5, 2.0),
        "near_weight": scatter_about(splits[4], (3, TRIS, CLUSTER_ROWS), (2.0 / (3 * CLUSTER_ROWS) ** 0.5), 0.21582031, ((1, 16), (2, 2))),
        "col_basis": scatter_about(splits[5], (LARGEST_RANK, TRIS), CLUSTER_ROWS ** -0.5, 0.1875, ((1, 16),)),
        "coupling": scatter_about(splits[6], (CLUSTER_TOTAL * LARGEST_RANK, CLUSTER_TOTAL * LARGEST_RANK), (CLUSTER_TOTAL * LARGEST_RANK) ** -0.5, 0.1875, ((0, 16),), jnp.float32),
        "cluster_row_factors": scatter_about(splits[7], (LARGEST_RANK, TRIS), (3.0 / LARGEST_RANK ** 0.5), 2.25, ((1, 16),), jnp.float32),
        "ranks": draw_ranks(jax.random.fold_in(splits[9], 71), 0),
    }


step_length = 0.5
damping = 0.5


def stress(deficit, near_weight, col_basis, coupling, cluster_row_factors, ranks):
    members = deficit.shape[0]
    grouped = deficit.reshape(members, CLUSTER_TOTAL, CLUSTER_ROWS)
    zero = jnp.zeros((members, 1, CLUSTER_ROWS), deficit.dtype)
    padded = jnp.concatenate([zero, grouped, zero], axis=1)
    windows = jnp.concatenate([padded[:, k:k + CLUSTER_TOTAL] for k in range(3)], axis=2)
    windows = jnp.transpose(windows, (1, 0, 2))
    blocks = jnp.transpose(near_weight.reshape(3, CLUSTER_TOTAL, CLUSTER_ROWS, CLUSTER_ROWS), (1, 2, 0, 3))
    blocks = blocks.reshape(CLUSTER_TOTAL, CLUSTER_ROWS, 3 * CLUSTER_ROWS)

    def one_cluster(item):
        window, block = item
        return jnp.dot(window, block.T, preferred_element_type=jnp.float32)

    near = lax.map(one_cluster, (windows, blocks))
    near = jnp.transpose(near, (1, 0, 2))
    rank_index = jnp.arange(LARGEST_RANK, dtype=jnp.int32)
    coef = jnp.einsum("mjr,kjr->mjk", grouped.astype(jnp.float32),
                      col_basis.reshape(LARGEST_RANK, CLUSTER_TOTAL, CLUSTER_ROWS).astype(jnp.float32),
                      precision=lax.Precision.HIGHEST)
    coef = jnp.where(rank_index[None, None, :] < ranks[None, :, None], coef, 0.0)
    cluster_index = jnp.arange(CLUSTER_TOTAL, dtype=jnp.int32)
    admissible = jnp.abs(cluster_index[:, None] - cluster_index[None, :]) > 1
    blocks_far = jnp.where(admissible[:, None, :, None], coupling.reshape(CLUSTER_TOTAL, LARGEST_RANK, CLUSTER_TOTAL, LARGEST_RANK), 0.0)
    compressed_sum = jnp.einsum("ikjl,mjl->mik", blocks_far, coef, precision=lax.Precision.HIGHEST)
    compressed_sum = jnp.where(rank_index[None, None, :] < ranks[None, :, None], compressed_sum, 0.0)
    distant_part = jnp.einsum("fel,leh->feh", compressed_sum, cluster_row_factors.reshape(LARGEST_RANK, CLUSTER_TOTAL, CLUSTER_ROWS),
                     precision=lax.Precision.HIGHEST)
    return (near + distant_part).reshape(members, CLUSTER_TOTAL * CLUSTER_ROWS)


def rates(current_logarithm, state_now, rate_coef, state_coef, operands):
    rate = jnp.exp(current_logarithm)
    deficit = (rate - 1.0).astype(jnp.bfloat16)
    stress_rate = stress(deficit, *operands)
    state_rate = jnp.exp(-state_now) - rate
    rate_rate = (stress_rate - state_coef * state_rate) / (rate_coef + damping * rate)
    return rate_rate, state_rate


def reference(log_rate, state, rate_coef, state_coef, near_weight, col_basis, coupling, cluster_row_factors, ranks):
    operands = (near_weight, col_basis, coupling, cluster_row_factors, ranks)
    rate_one, state_one = rates(log_rate, state, rate_coef, state_coef, operands)
    rate_two, state_two = rates(log_rate + step_length * rate_one, state + step_length * state_one,
                                rate_coef, state_coef, operands)
    log_rate_next = log_rate + 0.5 * step_length * (rate_one + rate_two)
    state_next = state + 0.5 * step_length * (state_one + state_two)
    return log_rate_next, state_next
```

```python
import functools
import math

import jax
import jax.numpy as jnp
from jax import lax
from jax.experimental import pallas as pl
from jax.experimental.pallas import tpu as pltpu
from jax.sharding import PartitionSpec as P

step_length = 0.5
damping = 0.5

MESH = pl.DeviceIdType.MESH
ROWS = (((1,), (1,)), ((), ()))


def split(value):
    high = value.astype(jnp.bfloat16)
    low = (value - high.astype(jnp.float32)).astype(jnp.bfloat16)
    return high, low


def kernel(
    n,
    group,
    log_rate_hbm,
    state_hbm,
    rate_coef_hbm,
    state_coef_hbm,
    near_hbm,
    basis_hbm,
    coupling_hbm,
    factors_hbm,
    ranks_ref,
    sums_out,
    log_rate_ref,
    basis_ref,
    friction,
    near_ref,
    coupling_ref,
    factors_ref,
    far_in,
    far_out,
    halves,
    halo,
    coef,
    part_send,
    part_recv,
    load_sem,
    upper_sem,
    halo_send_sem,
    partner_send_sem,
    halo_recv_sem,
    coef_send_sem,
    coef_recv_sem,
    part_recv_sem,
):
    me = lax.axis_index("cluster")
    core = lax.axis_index("ens")
    other = 1 - core
    levels = n // group
    level = me // group
    place = me % group
    members, rows = log_rate_ref.shape
    half = rows // 2
    widest = basis_ref.shape[0]

    barrier = pltpu.get_barrier_semaphore()

    def greet(cluster, ens):
        pl.semaphore_signal(barrier, inc=1, device_id=(cluster, ens), device_id_type=MESH)

    for d in range(1, group):
        greet(level * group + (place + d) % group, core)
    greet(me, other)

    @pl.when(me > 0)
    def _():
        greet(me - 1, other)

    @pl.when(me < n - 1)
    def _():
        greet(me + 1, other)

    @pl.when(jnp.logical_and(place == 0, level > 0))
    def _():
        greet(me - 1, core)

    for d in range(1, levels):

        @pl.when(level + d < levels)
        def _():
            for p in range(group):
                greet((level + d) * group + p, core)

    loads = [
        pltpu.make_async_copy(source, target, load_sem.at[i])
        for i, (source, target) in enumerate(
            (
                (log_rate_hbm, log_rate_ref),
                (basis_hbm, basis_ref),
                (coupling_hbm, coupling_ref),
                (factors_hbm, factors_ref),
                (near_hbm, near_ref),
            )
        )
    ]
    for load in loads:
        load.start()
    for i, source in enumerate((state_hbm, rate_coef_hbm, state_coef_hbm)):
        pltpu.make_async_copy(source, friction.at[i], load_sem.at[len(loads)]).start()

    own_rank = ranks_ref[0]
    lane = lax.broadcasted_iota(jnp.int32, (members, 2 * widest), 1)
    lane_rank = lax.rem(lane, widest)

    zero_half = jnp.zeros((members, half), halo.dtype)
    for section in range(2):

        @pl.when(me == 0)
        def _():
            for slot in range(2):
                halo[section, 0, slot] = zero_half

        @pl.when(me == n - 1)
        def _():
            for slot in range(2):
                halo[section, 2, slot] = zero_half

    def halo_copy(section, k, slot, cluster):
        ens = core if slot == 0 else other
        return pltpu.make_async_remote_copy(
            src_ref=halves.at[section, ens],
            dst_ref=halo.at[section, k, slot],
            send_sem=partner_send_sem if k == 1 else halo_send_sem.at[k // 2],
            recv_sem=halo_recv_sem.at[section, k],
            device_id=(cluster, ens),
            device_id_type=MESH,
        )

    def halo_arrival(section, k):
        return pltpu.make_async_remote_copy(
            src_ref=halo.at[section, k],
            dst_ref=halo.at[section, k],
            send_sem=halo_send_sem.at[k // 2],
            recv_sem=halo_recv_sem.at[section, k],
            device_id=(me, other),
            device_id_type=MESH,
        )

    def coef_copy(section, first, count, cluster):
        return pltpu.make_async_remote_copy(
            src_ref=coef.at[section, pl.ds(first, count)],
            dst_ref=coef.at[section, pl.ds(first, count)],
            send_sem=coef_send_sem,
            recv_sem=coef_recv_sem.at[section, level],
            device_id=(cluster, core),
            device_id_type=MESH,
        )

    def coef_arrival(section, source, count):
        return pltpu.make_async_remote_copy(
            src_ref=coef.at[section, pl.ds(source * group, count)],
            dst_ref=coef.at[section, pl.ds(source * group, count)],
            send_sem=coef_send_sem,
            recv_sem=coef_recv_sem.at[section, source],
            device_id=(me, other),
            device_id_type=MESH,
        )

    def part_copy(section):
        return pltpu.make_async_remote_copy(
            src_ref=part_send.at[section],
            dst_ref=part_recv.at[section],
            send_sem=partner_send_sem,
            recv_sem=part_recv_sem.at[section],
            device_id=(me, other),
            device_id_type=MESH,
        )

    def prepare():
        loads[2].wait()
        row = lax.broadcasted_iota(jnp.int32, (widest, 2 * widest), 0)
        kept = row < own_rank
        for j in range(n):
            block = coupling_ref[:, j * widest : (j + 1) * widest]
            block = jnp.concatenate([block, block], axis=1)
            block = jnp.where(jnp.logical_and(kept, jnp.abs(me - j) > 1), block, 0.0)
            high, low = split(block)
            columns = slice(2 * (j % group) * widest, 2 * (j % group + 1) * widest)
            far_in[j // group, 0:widest, columns] = high
            far_in[j // group, widest : 2 * widest, columns] = low
        loads[3].wait()
        high, low = split(factors_ref[...])
        far_out[0:widest] = high
        far_out[widest : 2 * widest] = high
        far_out[2 * widest : 3 * widest] = low
        far_out[3 * widest : 4 * widest] = low

    turn = jnp.where(2 * level < levels, 1, levels - 1)

    def rates(section, current_logarithm):
        rate = jnp.exp(current_logarithm)
        deficit = (rate - 1.0).astype(jnp.bfloat16)
        halves[section, 0] = deficit[:, :half]
        halves[section, 1] = deficit[:, half:]
        halo[section, 1, 0] = halves[section, core]
        if section == 0:
            loads[1].wait()
        basis = basis_ref[...]
        own = lax.dot_general(
            deficit,
            jnp.concatenate([basis, basis], axis=0),
            ROWS,
            preferred_element_type=jnp.float32,
        )
        own = jnp.where(lane_rank < own_rank, own, 0.0)
        high = own.astype(jnp.bfloat16).astype(jnp.float32)
        coef[section, me] = jnp.where(lane < widest, high, own - high).astype(jnp.bfloat16)

        if section == 0:
            greeted = (
                group * (level + 1)
                + jnp.where(me > 0, 1, 0)
                + jnp.where(me < n - 1, 1, 0)
                + jnp.where(jnp.logical_and(place == group - 1, level < levels - 1), 1, 0)
            )
            pl.semaphore_wait(barrier, greeted)

            for d in range(levels - 1, 0, -1):

                @pl.when(level >= d)
                def _():
                    pl.semaphore_signal(
                        upper_sem,
                        inc=1,
                        device_id=((level - d) * group + place, core),
                        device_id_type=MESH,
                    )

            for d in range(levels - 1, 0, -1):

                @pl.when(level >= d)
                def _():
                    for p in range(group):
                        coef_copy(section, me, 1, (level - d) * group + p).start()

            for d in range(1, group):
                coef_copy(section, me, 1, level * group + (place + d) % group).start()
        else:
            for j in range(n):

                @pl.when(j != me)
                def _():
                    coef_copy(section, me, 1, jnp.int32(j)).start()

        @pl.when(me > 0)
        def _():
            for slot in range(2):
                halo_copy(section, 2, slot, me - 1).start()

        @pl.when(me < n - 1)
        def _():
            for slot in range(2):
                halo_copy(section, 0, slot, me + 1).start()

        halo_copy(section, 1, 1, me).start()

        if section == 0:
            prepare()
            loads[4].wait()

        def near(k):
            columns = jnp.concatenate([halo[section, k, 0], halo[section, k, 1]], axis=0)
            return lax.dot_general(
                columns, near_ref[k], ROWS, preferred_element_type=jnp.float32
            )

        if section == 0:
            @pl.when(level < levels - 1)
            def _():
                coef_arrival(section, level, group - 1).wait_recv()
                pl.semaphore_wait(upper_sem, levels - 1 - level)
                for d in range(levels - 1, 0, -1):

                    @pl.when(level + d < levels)
                    def _():
                        coef_copy(
                            section, level * group, group, (level + d) * group + place
                        ).start()

        halo_copy(section, 1, 1, me).wait_recv()
        total = near(1)

        @pl.when(me > 0)
        def _():
            halo_arrival(section, 0).wait_recv()

        total = total + near(0)

        @pl.when(me < n - 1)
        def _():
            halo_arrival(section, 2).wait_recv()

        total = total + near(2)
        part_send[section] = total[members:]
        part_copy(section).start()

        if section == 0:

            @pl.when(level == levels - 1)
            def _():
                coef_arrival(section, level, group - 1).wait_recv()
        else:
            coef_arrival(section, level, group - 1).wait_recv()

        reduced = None
        for d in range(levels):
            source = (level + d * turn) % levels
            if d > 0:
                coef_arrival(section, source, group).wait_recv()
            coefs = coef[section, pl.ds(source * group, group)]
            coefs = jnp.concatenate([coefs[j] for j in range(group)], axis=1)
            term = lax.dot_general(
                coefs, far_in[source], ROWS, preferred_element_type=jnp.float32
            )
            reduced = term if reduced is None else reduced + term
        high, low = split(reduced)
        reduced = jnp.concatenate(
            [jnp.concatenate([high, high], axis=1), jnp.concatenate([low, low], axis=1)], axis=0
        )
        far = jnp.dot(reduced, far_out[...], preferred_element_type=jnp.float32)
        stress_rate = total[:members] + (far[:members] + far[members:])
        part_copy(section).wait_recv()
        return rate, stress_rate + part_recv[section]

    loads[0].wait()
    log_rate = log_rate_ref[...]
    rate, stress_one = rates(0, log_rate)
    pltpu.make_async_copy(friction, friction, load_sem.at[len(loads)]).wait()
    state, rate_coef, state_coef = friction[0], friction[1], friction[2]
    state_one = jnp.exp(-state) - rate
    rate_one = (stress_one - state_coef * state_one) / (rate_coef + damping * rate)
    second, stress_two = rates(1, log_rate + step_length * rate_one)
    state_two = jnp.exp(-(state + step_length * state_one)) - second
    rate_two = (stress_two - state_coef * state_two) / (rate_coef + damping * second)
    sums_out[0] = rate_one + rate_two
    sums_out[1] = state_one + state_two

    def sent(source, semaphore):
        pltpu.make_async_remote_copy(
            src_ref=source,
            dst_ref=source,
            send_sem=semaphore,
            recv_sem=part_recv_sem.at[0],
            device_id=(me, other),
            device_id_type=MESH,
        ).wait_send()

    sent(coef.at[:, pl.ds(0, n - 1)], coef_send_sem)

    @pl.when(me > 0)
    def _():
        sent(halves, halo_send_sem.at[1])

    @pl.when(me < n - 1)
    def _():
        sent(halves, halo_send_sem.at[0])

    for section in range(2):
        halo_copy(section, 1, 1, me).wait_send()
        part_copy(section).wait_send()


def finish(sums_ref, log_rate_ref, state_ref, log_rate_out, state_out):
    log_rate_out[...] = log_rate_ref[...] + 0.5 * step_length * sums_ref[0]
    state_out[...] = state_ref[...] + 0.5 * step_length * sums_ref[1]


def local(n, *args):
    log_rate, near_weight, col_basis, coupling, factors = (args[i] for i in (0, 4, 5, 6, 7))
    members, rows = log_rate.shape
    half = near_weight.shape[2]
    widest = col_basis.shape[0]
    group = max(d for d in range(1, math.isqrt(n) + 1) if n % d == 0)
    levels = n // group
    f32, bf16 = jnp.float32, jnp.bfloat16
    in_hbm = pl.BlockSpec(memory_space=pltpu.HBM)
    vmem = pl.BlockSpec(memory_space=pltpu.VMEM)
    smem = pl.BlockSpec(memory_space=pltpu.SMEM)
    sums = pl.pallas_call(
        functools.partial(kernel, n, group),
        out_shape=pltpu.VMEM((2, members, rows), f32),
        in_specs=[in_hbm] * 8 + [smem],
        out_specs=vmem,
        scratch_shapes=[
            pltpu.VMEM((members, rows), f32),
            pltpu.VMEM(col_basis.shape, bf16),
            pltpu.VMEM((3, members, rows), f32),
            pltpu.VMEM(near_weight.shape, bf16),
            pltpu.VMEM(coupling.shape, f32),
            pltpu.VMEM(factors.shape, f32),
            pltpu.VMEM((levels, 2 * widest, group * 2 * widest), bf16),
            pltpu.VMEM((4 * widest, rows), bf16),
            pltpu.VMEM((2, 2, members, half), bf16),
            pltpu.VMEM((2, 3, 2, members, half), bf16),
            pltpu.VMEM((2, n, members, 2 * widest), bf16),
            pltpu.VMEM((2, members, rows), f32),
            pltpu.VMEM((2, members, rows), f32),
            pltpu.SemaphoreType.DMA((6,)),
            pltpu.SemaphoreType.REGULAR,
            pltpu.SemaphoreType.DMA((2,)),
            pltpu.SemaphoreType.DMA,
            pltpu.SemaphoreType.DMA((2, 3)),
            pltpu.SemaphoreType.DMA,
            pltpu.SemaphoreType.DMA((2, levels)),
            pltpu.SemaphoreType.DMA((2,)),
        ],
        compiler_params=pltpu.CompilerParams(
            collective_id=0, has_side_effects=True, vmem_limit_bytes=60 * 1024 * 1024
        ),
    )(*args)
    return tuple(
        pl.pallas_call(
            finish,
            out_shape=[jax.ShapeDtypeStruct((members, rows), f32)] * 2,
            in_specs=[vmem] * 3,
            out_specs=[vmem] * 2,
            compiler_params=pltpu.CompilerParams(vmem_limit_bytes=1024 * 1024),
        )(sums, args[0], args[1])
    )


def solution(mesh):
    in_specs = (
        P("ens", "cluster"),
        P("ens", "cluster"),
        P("ens", "cluster"),
        P("ens", "cluster"),
        P(None, "cluster", "ens"),
        P(None, "cluster"),
        P("cluster", None),
        P(None, "cluster"),
        P("cluster"),
    )
    out_specs = (P("ens", "cluster"), P("ens", "cluster"))
    return jax.shard_map(
        functools.partial(local, mesh.shape["cluster"]),
        mesh=mesh,
        in_specs=in_specs,
        out_specs=out_specs,
        check_vma=False,
    )
```

```python
import functools
import math

import jax
import jax.numpy as jnp
from jax import lax
from jax.experimental import pallas as pl
from jax.experimental.pallas import tpu as pltpu
from jax.sharding import PartitionSpec as P

step_length = 0.5
damping = 0.5

MESH = pl.DeviceIdType.MESH
ROWS = (((1,), (1,)), ((), ()))


def split(value):
    high = value.astype(jnp.bfloat16)
    low = (value - high.astype(jnp.float32)).astype(jnp.bfloat16)
    return high, low


def kernel(
    n,
    group,
    log_rate_hbm,
    state_hbm,
    rate_coef_hbm,
    state_coef_hbm,
    near_hbm,
    basis_hbm,
    coupling_hbm,
    factors_hbm,
    ranks_ref,
    sums_out,
    log_rate_ref,
    basis_ref,
    friction,
    near_ref,
    coupling_ref,
    factors_ref,
    basis_turned,
    far_in,
    far_out,
    halves,
    halo,
    coef,
    part_send,
    part_recv,
    load_sem,
    last_sem,
    upper_sem,
    send_sem,
    halo_recv_sem,
    coef_recv_sem,
    part_recv_sem,
):
    me = lax.axis_index("cluster")
    core = lax.axis_index("ens")
    other = 1 - core
    levels = n // group
    level = me // group
    place = me % group
    members, rows = log_rate_ref.shape
    half = rows // 2
    widest = basis_ref.shape[0]

    barrier = pltpu.get_barrier_semaphore()

    def greet(cluster, ens):
        pl.semaphore_signal(barrier, inc=1, device_id=(cluster, ens), device_id_type=MESH)

    for d in range(1, group):
        greet(level * group + (place + d) % group, core)
    greet(me, other)

    @pl.when(me > 0)
    def _():
        greet(me - 1, other)

    @pl.when(me < n - 1)
    def _():
        greet(me + 1, other)

    @pl.when(jnp.logical_and(place == 0, level > 0))
    def _():
        greet(me - 1, core)

    for d in range(1, levels):

        @pl.when(level + d < levels)
        def _():
            for p in range(group):
                greet((level + d) * group + p, core)

    def of_bytes(count):
        tiles = count // (16 * 128)
        across = next(c for c in (1, 2, 4) if tiles % c == 0 and 8 * tiles // c <= near_ref.shape[0])
        return near_ref.at[pl.ds(0, 8 * tiles // across), pl.ds(0, 128 * across)]

    loads = (
        (log_rate_hbm, log_rate_ref, 0),
        (basis_hbm, basis_ref, 0),
        (coupling_hbm, coupling_ref, 1),
        (factors_hbm, factors_ref, 1),
        (state_hbm, friction.at[0], 1),
        (rate_coef_hbm, friction.at[1], 1),
        (state_coef_hbm, friction.at[2], 1),
        (near_hbm, near_ref, 2),
    )
    for source, target, i in loads:
        pltpu.make_async_copy(source, target, load_sem.at[i]).start()

    def loaded(i):
        count = sum(math.prod(t.shape) * t.dtype.itemsize for _, t, j in loads if i == j)
        pltpu.make_async_copy(of_bytes(count), of_bytes(count), load_sem.at[i]).wait()

    own_rank = ranks_ref[0]
    lane = lax.broadcasted_iota(jnp.int32, (members, 2 * widest), 1)
    lane_rank = lax.rem(lane, widest)

    zero_half = jnp.zeros((members, half), halo.dtype)
    for section in range(2):

        @pl.when(me == 0)
        def _():
            for slot in range(2):
                halo[section, 0, slot] = zero_half

        @pl.when(me == n - 1)
        def _():
            for slot in range(2):
                halo[section, 2, slot] = zero_half

    def halo_copy(section, k, slot, cluster):
        ens = core if slot == 0 else other
        return pltpu.make_async_remote_copy(
            src_ref=halves.at[section, ens],
            dst_ref=halo.at[section, k, slot],
            send_sem=send_sem,
            recv_sem=halo_recv_sem.at[section, k],
            device_id=(cluster, ens),
            device_id_type=MESH,
        )

    def halo_arrival(section, k):
        return pltpu.make_async_remote_copy(
            src_ref=halo.at[section, k],
            dst_ref=halo.at[section, k],
            send_sem=send_sem,
            recv_sem=halo_recv_sem.at[section, k],
            device_id=(me, other),
            device_id_type=MESH,
        )

    def coef_copy(section, first, count, cluster):
        return pltpu.make_async_remote_copy(
            src_ref=coef.at[section, pl.ds(first, count)],
            dst_ref=coef.at[section, pl.ds(first, count)],
            send_sem=send_sem,
            recv_sem=coef_recv_sem.at[section, level],
            device_id=(cluster, core),
            device_id_type=MESH,
        )

    def coef_arrival(section, source, count):
        return pltpu.make_async_remote_copy(
            src_ref=coef.at[section, pl.ds(source * group, count)],
            dst_ref=coef.at[section, pl.ds(source * group, count)],
            send_sem=send_sem,
            recv_sem=coef_recv_sem.at[section, source],
            device_id=(me, other),
            device_id_type=MESH,
        )

    def part_copy(section):
        return pltpu.make_async_remote_copy(
            src_ref=part_send.at[section],
            dst_ref=part_recv.at[section],
            send_sem=send_sem,
            recv_sem=part_recv_sem.at[section],
            device_id=(me, other),
            device_id_type=MESH,
        )

    def prepare():
        turned = jnp.transpose(basis_ref[...].astype(jnp.float32)).astype(jnp.bfloat16)
        basis_turned[...] = jnp.concatenate([turned, turned], axis=1)
        loaded(1)
        row = lax.broadcasted_iota(jnp.int32, (widest, group * widest), 0)
        cluster = lax.broadcasted_iota(jnp.int32, (widest, group * widest), 1) // widest
        for source in range(levels):
            block = coupling_ref[:, source * group * widest : (source + 1) * group * widest]
            far = jnp.abs(me - source * group - cluster) > 1
            block = jnp.where(jnp.logical_and(row < own_rank, far), block, 0.0)
            high, low = split(jnp.transpose(block))
            block = jnp.concatenate([high, low], axis=1)
            for j in range(group):
                piece = block[j * widest : (j + 1) * widest]
                far_in[source, 2 * j * widest : (2 * j + 1) * widest] = piece
                far_in[source, (2 * j + 1) * widest : 2 * (j + 1) * widest] = piece
        high, low = split(factors_ref[...])
        far_out[0:widest] = high
        far_out[widest : 2 * widest] = high
        far_out[2 * widest : 3 * widest] = low
        far_out[3 * widest : 4 * widest] = low

    turn = jnp.where(2 * level < levels, 1, levels - 1)

    def enter():
        greeted = (
            group * (level + 1)
            + jnp.where(me > 0, 1, 0)
            + jnp.where(me < n - 1, 1, 0)
            + jnp.where(jnp.logical_and(place == group - 1, level < levels - 1), 1, 0)
        )
        pl.semaphore_wait(barrier, greeted)

        def answer(semaphore, cluster):
            pl.semaphore_signal(semaphore, inc=1, device_id=(cluster, core), device_id_type=MESH)

        for d in range(levels - 1, 0, -1):

            @pl.when(level >= d if d > 1 else jnp.logical_and(level > 0, level < levels - 1))
            def _():
                answer(upper_sem, (level - d) * group + place)

        @pl.when(level == levels - 1)
        def _():
            for d in range(group):
                answer(last_sem, (level - 1) * group + (place + d) % group)

    def rates(section, current_logarithm, early):
        rate = jnp.exp(current_logarithm)
        deficit = (rate - 1.0).astype(jnp.bfloat16)
        halves[section, 0] = deficit[:, :half]
        halves[section, 1] = deficit[:, half:]
        halo[section, 1, 0] = halves[section, core]
        if section == 0:
            basis = basis_ref[...]
            own = lax.dot_general(
                deficit,
                jnp.concatenate([basis, basis], axis=0),
                ROWS,
                preferred_element_type=jnp.float32,
            )
        else:
            own = jnp.dot(deficit, basis_turned[...], preferred_element_type=jnp.float32)
        own = jnp.where(lane_rank < own_rank, own, 0.0)
        high = own.astype(jnp.bfloat16).astype(jnp.float32)
        coef[section, me] = jnp.where(lane < widest, high, own - high).astype(jnp.bfloat16)

        if section == 0:

            @pl.when(me < n - 1)
            def _():
                enter()

            for d in range(levels - 1, 0, -1):

                @pl.when(level >= d)
                def _():
                    for p in range(group):
                        coef_copy(section, me, 1, (level - d) * group + p).start()

            for d in range(1, group):
                coef_copy(section, me, 1, level * group + (place + d) % group).start()
        else:
            for j in range(n):

                @pl.when(j != me)
                def _():
                    coef_copy(section, me, 1, jnp.int32(j)).start()

        @pl.when(me > 0)
        def _():
            for slot in range(2):
                halo_copy(section, 2, slot, me - 1).start()

        @pl.when(me < n - 1)
        def _():
            for slot in range(2):
                halo_copy(section, 0, slot, me + 1).start()

        halo_copy(section, 1, 1, me).start()

        if section == 0:
            prepare()
            loaded(2)

        def near(k):
            columns = jnp.concatenate([halo[section, k, 0], halo[section, k, 1]], axis=0)
            return lax.dot_general(
                columns, near_ref[k * rows : (k + 1) * rows], ROWS, preferred_element_type=jnp.float32
            )

        if section == 0:
            @pl.when(level == levels - 2)
            def _():
                pl.semaphore_wait(last_sem, group)
                for d in range(group):
                    coef_copy(section, me, 1, (level + 1) * group + (place + d) % group).start()

            @pl.when(level < levels - 2)
            def _():
                coef_arrival(section, level, group - 1).wait_recv()
                pl.semaphore_wait(upper_sem, levels - 1 - level)
                for d in range(levels - 1, 0, -1):

                    @pl.when(level + d < levels)
                    def _():
                        coef_copy(
                            section, level * group, group, (level + d) * group + place
                        ).start()

        halo_copy(section, 1, 1, me).wait_recv()
        total = near(1)

        @pl.when(me > 0)
        def _():
            halo_arrival(section, 0).wait_recv()

        total = total + near(0)

        @pl.when(me < n - 1)
        def _():
            halo_arrival(section, 2).wait_recv()

        total = total + near(2)
        part_send[section] = total[members:]
        part_copy(section).start()
        early = early(rate)

        if section == 0:

            @pl.when(level >= levels - 2)
            def _():
                coef_arrival(section, level, group - 1).wait_recv()
        else:
            coef_arrival(section, level, group - 1).wait_recv()

        reduced = None
        for d in range(levels):
            source = (level + d * turn) % levels
            if section == 0 and d > 1:
                source = jnp.where(level == levels - 1, d - 2, source)
            if d > 0:
                coef_arrival(section, source, group).wait_recv()
            coefs = coef[section, pl.ds(source * group, group)]
            coefs = jnp.concatenate([coefs[j] for j in range(group)], axis=1)
            term = jnp.dot(coefs, far_in[source], preferred_element_type=jnp.float32)
            reduced = term if reduced is None else reduced + term
        high, low = split(reduced)
        reduced = jnp.concatenate(
            [jnp.concatenate([high, high], axis=1), jnp.concatenate([low, low], axis=1)], axis=0
        )
        far = jnp.concatenate(
            [
                jnp.dot(reduced, far_out[:, :half], preferred_element_type=jnp.float32),
                jnp.dot(reduced, far_out[:, half:], preferred_element_type=jnp.float32),
            ],
            axis=1,
        )
        stress_rate = total[:members] + (far[:members] + far[members:])
        part_copy(section).wait_recv()
        return stress_rate + part_recv[section], early

    @pl.when(me == n - 1)
    def _():
        enter()

    loaded(0)
    log_rate = log_rate_ref[...]

    def apart(rate, state, state_coef, rate_coef):
        state_rate = jnp.exp(-state) - rate
        return state_rate, state_coef * state_rate, 1.0 / (rate_coef + damping * rate)

    def early_one(rate):
        return apart(rate, friction[0], friction[2], friction[1])

    stress_one, (state_one, healing, inverse) = rates(0, log_rate, early_one)
    rate_one = (stress_one - healing) * inverse

    def early_two(rate):
        return apart(rate, friction[0] + step_length * state_one, friction[2], friction[1])

    stress_two, (state_two, healing, inverse) = rates(
        1, log_rate + step_length * rate_one, early_two
    )
    sums_out[0] = rate_one + (stress_two - healing) * inverse
    sums_out[1] = state_one + state_two

    sent = 2 * (n - 1) * members * 2 * widest * 2 + 2 * (members * half * 2 + members * rows * 4)
    side = 2 * 2 * members * half * 2

    @pl.when(jnp.logical_and(me > 0, me < n - 1))
    def _():
        pltpu.make_async_copy(of_bytes(sent + 2 * side), of_bytes(sent + 2 * side), send_sem).wait()

    @pl.when(jnp.logical_or(me == 0, me == n - 1))
    def _():
        pltpu.make_async_copy(of_bytes(sent + side), of_bytes(sent + side), send_sem).wait()


def finish(sums_ref, log_rate_ref, state_ref, log_rate_out, state_out):
    log_rate_out[...] = log_rate_ref[...] + 0.5 * step_length * sums_ref[0]
    state_out[...] = state_ref[...] + 0.5 * step_length * sums_ref[1]


def local(n, *args):
    log_rate, near_weight, col_basis, coupling, factors = (args[i] for i in (0, 4, 5, 6, 7))
    members, rows = log_rate.shape
    half = near_weight.shape[2]
    widest = col_basis.shape[0]
    group = max(d for d in range(1, math.isqrt(n) + 1) if n % d == 0)
    levels = n // group
    f32, bf16 = jnp.float32, jnp.bfloat16
    in_hbm = pl.BlockSpec(memory_space=pltpu.HBM)
    vmem = pl.BlockSpec(memory_space=pltpu.VMEM)
    smem = pl.BlockSpec(memory_space=pltpu.SMEM)
    sums = pl.pallas_call(
        functools.partial(kernel, n, group),
        out_shape=pltpu.VMEM((2, members, rows), f32),
        in_specs=[in_hbm] * 8 + [smem],
        out_specs=vmem,
        scratch_shapes=[
            pltpu.VMEM((members, rows), f32),
            pltpu.VMEM(col_basis.shape, bf16),
            pltpu.VMEM((3, members, rows), f32),
            pltpu.VMEM((3 * rows, half), bf16),
            pltpu.VMEM(coupling.shape, f32),
            pltpu.VMEM(factors.shape, f32),
            pltpu.VMEM((rows, 2 * widest), bf16),
            pltpu.VMEM((levels, group * 2 * widest, 2 * widest), bf16),
            pltpu.VMEM((4 * widest, rows), bf16),
            pltpu.VMEM((2, 2, members, half), bf16),
            pltpu.VMEM((2, 3, 2, members, half), bf16),
            pltpu.VMEM((2, n, members, 2 * widest), bf16),
            pltpu.VMEM((2, members, rows), f32),
            pltpu.VMEM((2, members, rows), f32),
            pltpu.SemaphoreType.DMA((3,)),
            pltpu.SemaphoreType.REGULAR,
            pltpu.SemaphoreType.REGULAR,
            pltpu.SemaphoreType.DMA,
            pltpu.SemaphoreType.DMA((2, 3)),
            pltpu.SemaphoreType.DMA((2, levels)),
            pltpu.SemaphoreType.DMA((2,)),
        ],
        compiler_params=pltpu.CompilerParams(
            collective_id=0, has_side_effects=True, vmem_limit_bytes=60 * 1024 * 1024
        ),
    )(*args[:4], near_weight.reshape(3 * rows, half), *args[5:])
    return tuple(
        pl.pallas_call(
            finish,
            out_shape=[jax.ShapeDtypeStruct((members, rows), f32)] * 2,
            in_specs=[vmem] * 3,
            out_specs=[vmem] * 2,
            compiler_params=pltpu.CompilerParams(vmem_limit_bytes=1024 * 1024),
        )(sums, args[0], args[1])
    )


def solution(mesh):
    in_specs = (
        P("ens", "cluster"),
        P("ens", "cluster"),
        P("ens", "cluster"),
        P("ens", "cluster"),
        P(None, "cluster", "ens"),
        P(None, "cluster"),
        P("cluster", None),
        P(None, "cluster"),
        P("cluster"),
    )
    out_specs = (P("ens", "cluster"), P("ens", "cluster"))
    return jax.shard_map(
        functools.partial(local, mesh.shape["cluster"]),
        mesh=mesh,
        in_specs=in_specs,
        out_specs=out_specs,
        check_vma=False,
    )
```

```python
import functools
import math

import jax
import jax.numpy as jnp
from jax import lax
from jax.experimental import pallas as pl
from jax.experimental.pallas import tpu as pltpu
from jax.sharding import PartitionSpec as P

step_length = 0.5
damping = 0.5

MESH = pl.DeviceIdType.MESH
ROWS = (((1,), (1,)), ((), ()))


def split(value):
    high = value.astype(jnp.bfloat16)
    low = (value - high.astype(jnp.float32)).astype(jnp.bfloat16)
    return high, low


def kernel(
    n,
    group,
    log_rate_hbm,
    state_hbm,
    rate_coef_hbm,
    state_coef_hbm,
    near_hbm,
    basis_hbm,
    coupling_hbm,
    factors_hbm,
    ranks_ref,
    next_out,
    log_rate_ref,
    basis_ref,
    friction,
    near_ref,
    coupling_ref,
    factors_ref,
    basis_turned,
    far_in,
    far_out,
    halves,
    halo,
    coef,
    part_send,
    part_recv,
    load_sem,
    last_sem,
    upper_sem,
    send_sem,
    halo_recv_sem,
    coef_recv_sem,
    part_recv_sem,
):
    me = lax.axis_index("cluster")
    core = lax.axis_index("ens")
    other = 1 - core
    levels = n // group
    level = me // group
    place = me % group
    members, rows = log_rate_ref.shape
    half = rows // 2
    widest = basis_ref.shape[0]

    barrier = pltpu.get_barrier_semaphore()

    def greet(cluster, ens):
        pl.semaphore_signal(barrier, inc=1, device_id=(cluster, ens), device_id_type=MESH)

    for d in range(1, group):
        greet(level * group + (place + d) % group, core)
    greet(me, other)

    @pl.when(me > 0)
    def _():
        greet(me - 1, other)

    @pl.when(me < n - 1)
    def _():
        greet(me + 1, other)

    @pl.when(jnp.logical_and(place == 0, level > 0))
    def _():
        greet(me - 1, core)

    for d in range(1, levels):

        @pl.when(level + d < levels)
        def _():
            for p in range(group):
                greet((level + d) * group + p, core)

    def of_bytes(count):
        tiles = count // (16 * 128)
        across = next(c for c in (1, 2, 4) if tiles % c == 0 and 8 * tiles // c <= near_ref.shape[0])
        return near_ref.at[pl.ds(0, 8 * tiles // across), pl.ds(0, 128 * across)]

    loads = (
        (log_rate_hbm, log_rate_ref, 0),
        (basis_hbm, basis_ref, 0),
        (coupling_hbm, coupling_ref, 1),
        (factors_hbm, factors_ref, 1),
        (state_hbm, friction.at[0], 1),
        (rate_coef_hbm, friction.at[1], 1),
        (state_coef_hbm, friction.at[2], 1),
        (near_hbm, near_ref, 2),
    )
    for source, target, i in loads:
        pltpu.make_async_copy(source, target, load_sem.at[i]).start()

    def loaded(i):
        count = sum(math.prod(t.shape) * t.dtype.itemsize for _, t, j in loads if i == j)
        pltpu.make_async_copy(of_bytes(count), of_bytes(count), load_sem.at[i]).wait()

    own_rank = ranks_ref[0]
    lane = lax.broadcasted_iota(jnp.int32, (members, 2 * widest), 1)
    lane_rank = lax.rem(lane, widest)

    zero_half = jnp.zeros((members, half), halo.dtype)
    for section in range(2):

        @pl.when(me == 0)
        def _():
            for slot in range(2):
                halo[section, 0, slot] = zero_half

        @pl.when(me == n - 1)
        def _():
            for slot in range(2):
                halo[section, 2, slot] = zero_half

    def halo_copy(section, k, slot, cluster):
        ens = core if slot == 0 else other
        return pltpu.make_async_remote_copy(
            src_ref=halves.at[section, ens],
            dst_ref=halo.at[section, k, slot],
            send_sem=send_sem,
            recv_sem=halo_recv_sem.at[section, k],
            device_id=(cluster, ens),
            device_id_type=MESH,
        )

    def halo_arrival(section, k):
        return pltpu.make_async_remote_copy(
            src_ref=halo.at[section, k],
            dst_ref=halo.at[section, k],
            send_sem=send_sem,
            recv_sem=halo_recv_sem.at[section, k],
            device_id=(me, other),
            device_id_type=MESH,
        )

    def coef_copy(section, first, count, cluster):
        return pltpu.make_async_remote_copy(
            src_ref=coef.at[section, pl.ds(first, count)],
            dst_ref=coef.at[section, pl.ds(first, count)],
            send_sem=send_sem,
            recv_sem=coef_recv_sem.at[section, level],
            device_id=(cluster, core),
            device_id_type=MESH,
        )

    def coef_arrival(section, source, count):
        return pltpu.make_async_remote_copy(
            src_ref=coef.at[section, pl.ds(source * group, count)],
            dst_ref=coef.at[section, pl.ds(source * group, count)],
            send_sem=send_sem,
            recv_sem=coef_recv_sem.at[section, source],
            device_id=(me, other),
            device_id_type=MESH,
        )

    def part_copy(section):
        return pltpu.make_async_remote_copy(
            src_ref=part_send.at[section],
            dst_ref=part_recv.at[section],
            send_sem=send_sem,
            recv_sem=part_recv_sem.at[section],
            device_id=(me, other),
            device_id_type=MESH,
        )

    def prepare():
        turned = jnp.transpose(basis_ref[...].astype(jnp.float32)).astype(jnp.bfloat16)
        basis_turned[...] = jnp.concatenate([turned, turned], axis=1)
        loaded(1)
        row = lax.broadcasted_iota(jnp.int32, (widest, group * widest), 0)
        cluster = lax.broadcasted_iota(jnp.int32, (widest, group * widest), 1) // widest
        for source in range(levels):
            block = coupling_ref[:, source * group * widest : (source + 1) * group * widest]
            far = jnp.abs(me - source * group - cluster) > 1
            block = jnp.where(jnp.logical_and(row < own_rank, far), block, 0.0)
            high, low = split(jnp.transpose(block))
            block = jnp.concatenate([high, low], axis=1)
            for j in range(group):
                piece = block[j * widest : (j + 1) * widest]
                far_in[source, 2 * j * widest : (2 * j + 1) * widest] = piece
                far_in[source, (2 * j + 1) * widest : 2 * (j + 1) * widest] = piece
        high, low = split(factors_ref[...])
        far_out[0:widest] = high
        far_out[widest : 2 * widest] = high
        far_out[2 * widest : 3 * widest] = low
        far_out[3 * widest : 4 * widest] = low

    turn = jnp.where(2 * level < levels, 1, levels - 1)

    def enter():
        greeted = (
            group * (level + 1)
            + jnp.where(me > 0, 1, 0)
            + jnp.where(me < n - 1, 1, 0)
            + jnp.where(jnp.logical_and(place == group - 1, level < levels - 1), 1, 0)
        )
        pl.semaphore_wait(barrier, greeted)

        def answer(semaphore, cluster):
            pl.semaphore_signal(semaphore, inc=1, device_id=(cluster, core), device_id_type=MESH)

        for d in range(levels - 1, 0, -1):

            @pl.when(level >= d if d > 1 else jnp.logical_and(level > 0, level < levels - 1))
            def _():
                answer(upper_sem, (level - d) * group + place)

        @pl.when(level == levels - 1)
        def _():
            for d in range(group):
                answer(last_sem, (level - 1) * group + (place + d) % group)

    def rates(section, current_logarithm, early):
        rate = jnp.exp(current_logarithm)
        deficit = (rate - 1.0).astype(jnp.bfloat16)
        halves[section, 0] = deficit[:, :half]
        halves[section, 1] = deficit[:, half:]
        halo[section, 1, 0] = halves[section, core]
        if section == 0:
            basis = basis_ref[...]
            own = lax.dot_general(
                deficit,
                jnp.concatenate([basis, basis], axis=0),
                ROWS,
                preferred_element_type=jnp.float32,
            )
        else:
            own = jnp.dot(deficit, basis_turned[...], preferred_element_type=jnp.float32)
        own = jnp.where(lane_rank < own_rank, own, 0.0)
        high = own.astype(jnp.bfloat16).astype(jnp.float32)
        coef[section, me] = jnp.where(lane < widest, high, own - high).astype(jnp.bfloat16)

        if section == 0:

            @pl.when(me < n - 1)
            def _():
                enter()

            for d in range(levels - 1, 0, -1):

                @pl.when(level >= d)
                def _():
                    for p in range(group):
                        coef_copy(section, me, 1, (level - d) * group + p).start()

            for d in range(1, group):
                coef_copy(section, me, 1, level * group + (place + d) % group).start()
        else:
            for j in range(n):

                @pl.when(j != me)
                def _():
                    coef_copy(section, me, 1, jnp.int32(j)).start()

        @pl.when(me > 0)
        def _():
            for slot in range(2):
                halo_copy(section, 2, slot, me - 1).start()

        @pl.when(me < n - 1)
        def _():
            for slot in range(2):
                halo_copy(section, 0, slot, me + 1).start()

        halo_copy(section, 1, 1, me).start()

        if section == 0:
            prepare()
            loaded(2)

        def near(k):
            columns = jnp.concatenate([halo[section, k, 0], halo[section, k, 1]], axis=0)
            return lax.dot_general(
                columns, near_ref[k * rows : (k + 1) * rows], ROWS, preferred_element_type=jnp.float32
            )

        if section == 0:
            @pl.when(level == levels - 2)
            def _():
                pl.semaphore_wait(last_sem, group)
                for d in range(group):
                    coef_copy(section, me, 1, (level + 1) * group + (place + d) % group).start()

            @pl.when(level < levels - 2)
            def _():
                coef_arrival(section, level, group - 1).wait_recv()
                pl.semaphore_wait(upper_sem, levels - 1 - level)
                for d in range(levels - 1, 0, -1):

                    @pl.when(level + d < levels)
                    def _():
                        coef_copy(
                            section, level * group, group, (level + d) * group + place
                        ).start()

        halo_copy(section, 1, 1, me).wait_recv()
        total = near(1)

        @pl.when(me > 0)
        def _():
            halo_arrival(section, 0).wait_recv()

        total = total + near(0)

        @pl.when(me < n - 1)
        def _():
            halo_arrival(section, 2).wait_recv()

        total = total + near(2)
        part_send[section] = total[members:]
        part_copy(section).start()
        early = early(rate)

        if section == 0:

            @pl.when(level >= levels - 2)
            def _():
                coef_arrival(section, level, group - 1).wait_recv()
        else:
            coef_arrival(section, level, group - 1).wait_recv()

        reduced = None
        for d in range(levels):
            source = (level + d * turn) % levels
            if section == 0 and d > 1:
                source = jnp.where(level == levels - 1, d - 2, source)
            if d > 0:
                coef_arrival(section, source, group).wait_recv()
            coefs = coef[section, pl.ds(source * group, group)]
            coefs = jnp.concatenate([coefs[j] for j in range(group)], axis=1)
            term = jnp.dot(coefs, far_in[source], preferred_element_type=jnp.float32)
            reduced = term if reduced is None else reduced + term
        high, low = split(reduced)
        reduced = jnp.concatenate(
            [jnp.concatenate([high, high], axis=1), jnp.concatenate([low, low], axis=1)], axis=0
        )
        far = jnp.concatenate(
            [
                jnp.dot(reduced, far_out[:, :half], preferred_element_type=jnp.float32),
                jnp.dot(reduced, far_out[:, half:], preferred_element_type=jnp.float32),
            ],
            axis=1,
        )
        stress_rate = total[:members] + (far[:members] + far[members:])
        part_copy(section).wait_recv()
        return stress_rate + part_recv[section], early

    @pl.when(me == n - 1)
    def _():
        enter()

    loaded(0)
    log_rate = log_rate_ref[...]

    def apart(rate, state, state_coef, rate_coef):
        state_rate = jnp.exp(-state) - rate
        return state_rate, state_coef * state_rate, 1.0 / (rate_coef + damping * rate)

    def early_one(rate):
        return apart(rate, friction[0], friction[2], friction[1])

    stress_one, (state_one, healing, inverse) = rates(0, log_rate, early_one)
    rate_one = (stress_one - healing) * inverse

    def early_two(rate):
        return apart(rate, friction[0] + step_length * state_one, friction[2], friction[1])

    stress_two, (state_two, healing, inverse) = rates(
        1, log_rate + step_length * rate_one, early_two
    )
    next_out[0] = log_rate + 0.5 * step_length * (rate_one + (stress_two - healing) * inverse)
    next_out[1] = friction[0] + 0.5 * step_length * (state_one + state_two)

    sent = 2 * (n - 1) * members * 2 * widest * 2 + 2 * (members * half * 2 + members * rows * 4)
    side = 2 * 2 * members * half * 2

    @pl.when(jnp.logical_and(me > 0, me < n - 1))
    def _():
        pltpu.make_async_copy(of_bytes(sent + 2 * side), of_bytes(sent + 2 * side), send_sem).wait()

    @pl.when(jnp.logical_or(me == 0, me == n - 1))
    def _():
        pltpu.make_async_copy(of_bytes(sent + side), of_bytes(sent + side), send_sem).wait()


def finish(next_ref, log_rate_out, state_out, sem):
    copies = [
        pltpu.make_async_copy(next_ref.at[i], target, sem.at[i])
        for i, target in enumerate((log_rate_out, state_out))
    ]
    for copy in copies:
        copy.start()
    for copy in copies:
        copy.wait()


def local(n, *args):
    log_rate, near_weight, col_basis, coupling, factors = (args[i] for i in (0, 4, 5, 6, 7))
    members, rows = log_rate.shape
    half = near_weight.shape[2]
    widest = col_basis.shape[0]
    group = max(d for d in range(1, math.isqrt(n) + 1) if n % d == 0)
    levels = n // group
    f32, bf16 = jnp.float32, jnp.bfloat16
    in_hbm = pl.BlockSpec(memory_space=pltpu.HBM)
    vmem = pl.BlockSpec(memory_space=pltpu.VMEM)
    smem = pl.BlockSpec(memory_space=pltpu.SMEM)
    both = pl.pallas_call(
        functools.partial(kernel, n, group),
        out_shape=pltpu.VMEM((2, members, rows), f32),
        in_specs=[in_hbm] * 8 + [smem],
        out_specs=vmem,
        scratch_shapes=[
            pltpu.VMEM((members, rows), f32),
            pltpu.VMEM(col_basis.shape, bf16),
            pltpu.VMEM((3, members, rows), f32),
            pltpu.VMEM((3 * rows, half), bf16),
            pltpu.VMEM(coupling.shape, f32),
            pltpu.VMEM(factors.shape, f32),
            pltpu.VMEM((rows, 2 * widest), bf16),
            pltpu.VMEM((levels, group * 2 * widest, 2 * widest), bf16),
            pltpu.VMEM((4 * widest, rows), bf16),
            pltpu.VMEM((2, 2, members, half), bf16),
            pltpu.VMEM((2, 3, 2, members, half), bf16),
            pltpu.VMEM((2, n, members, 2 * widest), bf16),
            pltpu.VMEM((2, members, rows), f32),
            pltpu.VMEM((2, members, rows), f32),
            pltpu.SemaphoreType.DMA((3,)),
            pltpu.SemaphoreType.REGULAR,
            pltpu.SemaphoreType.REGULAR,
            pltpu.SemaphoreType.DMA,
            pltpu.SemaphoreType.DMA((2, 3)),
            pltpu.SemaphoreType.DMA((2, levels)),
            pltpu.SemaphoreType.DMA((2,)),
        ],
        compiler_params=pltpu.CompilerParams(
            collective_id=0, has_side_effects=True, vmem_limit_bytes=60 * 1024 * 1024
        ),
    )(*args[:4], near_weight.reshape(3 * rows, half), *args[5:])
    return tuple(
        pl.pallas_call(
            finish,
            out_shape=[jax.ShapeDtypeStruct((members, rows), f32)] * 2,
            in_specs=[vmem],
            out_specs=[in_hbm] * 2,
            scratch_shapes=[pltpu.SemaphoreType.DMA((2,))],
            compiler_params=pltpu.CompilerParams(vmem_limit_bytes=1024 * 1024),
        )(both)
    )


def solution(mesh):
    in_specs = (
        P("ens", "cluster"),
        P("ens", "cluster"),
        P("ens", "cluster"),
        P("ens", "cluster"),
        P(None, "cluster", "ens"),
        P(None, "cluster"),
        P("cluster", None),
        P(None, "cluster"),
        P("cluster"),
    )
    out_specs = (P("ens", "cluster"), P("ens", "cluster"))
    return jax.shard_map(
        functools.partial(local, mesh.shape["cluster"]),
        mesh=mesh,
        in_specs=in_specs,
        out_specs=out_specs,
        check_vma=False,
    )
```

```python
import functools
import math

import jax
import jax.numpy as jnp
from jax import lax
from jax.experimental import pallas as pl
from jax.experimental.pallas import tpu as pltpu
from jax.sharding import PartitionSpec as P

step_length = 0.5
damping = 0.5

MESH = pl.DeviceIdType.MESH
ROWS = (((1,), (1,)), ((), ()))


def split(value):
    high = value.astype(jnp.bfloat16)
    low = (value - high.astype(jnp.float32)).astype(jnp.bfloat16)
    return high, low


def kernel(
    n,
    group,
    log_rate_hbm,
    state_hbm,
    rate_coef_hbm,
    state_coef_hbm,
    near_hbm,
    basis_hbm,
    coupling_hbm,
    factors_hbm,
    ranks_ref,
    next_out,
    log_rate_ref,
    basis_ref,
    friction,
    near_ref,
    coupling_ref,
    factors_ref,
    basis_turned,
    far_in,
    far_out,
    halves,
    halo,
    coef,
    part_send,
    part_recv,
    load_sem,
    answer_sem,
    send_sem,
    halo_recv_sem,
    coef_recv_sem,
    part_recv_sem,
):
    me = lax.axis_index("cluster")
    core = lax.axis_index("ens")
    other = 1 - core
    levels = n // group
    level = me // group
    place = me % group
    members, rows = log_rate_ref.shape
    half = rows // 2
    widest = basis_ref.shape[0]

    barrier = pltpu.get_barrier_semaphore()

    def greet(cluster, ens):
        pl.semaphore_signal(barrier, inc=1, device_id=(cluster, ens), device_id_type=MESH)

    for d in range(1, group):
        greet(level * group + (place + d) % group, core)
    greet(me, other)

    @pl.when(me > 0)
    def _():
        greet(me - 1, other)

    @pl.when(me < n - 1)
    def _():
        greet(me + 1, other)

    @pl.when(jnp.logical_and(place == 0, level > 0))
    def _():
        greet(me - 1, core)

    for d in range(1, levels):

        @pl.when(level + d < levels)
        def _():
            for p in range(group):
                greet((level + d) * group + p, core)

    def of_bytes(count):
        tiles = count // (16 * 128)
        across = next(c for c in (1, 2, 4) if tiles % c == 0 and 8 * tiles // c <= near_ref.shape[0])
        return near_ref.at[pl.ds(0, 8 * tiles // across), pl.ds(0, 128 * across)]

    loads = (
        (log_rate_hbm, log_rate_ref, 0),
        (basis_hbm, basis_ref, 0),
        (coupling_hbm, coupling_ref, 1),
        (factors_hbm, factors_ref, 1),
        (state_hbm, friction.at[0], 1),
        (rate_coef_hbm, friction.at[1], 1),
        (state_coef_hbm, friction.at[2], 1),
        (near_hbm, near_ref, 2),
    )
    for source, target, i in loads:
        pltpu.make_async_copy(source, target, load_sem.at[i]).start()

    def loaded(i):
        count = sum(math.prod(t.shape) * t.dtype.itemsize for _, t, j in loads if i == j)
        pltpu.make_async_copy(of_bytes(count), of_bytes(count), load_sem.at[i]).wait()

    own_rank = ranks_ref[0]
    lane = lax.broadcasted_iota(jnp.int32, (members, 2 * widest), 1)
    lane_rank = lax.rem(lane, widest)

    zero_half = jnp.zeros((members, half), halo.dtype)
    for section in range(2):

        @pl.when(me == 0)
        def _():
            for slot in range(2):
                halo[section, 0, slot] = zero_half

        @pl.when(me == n - 1)
        def _():
            for slot in range(2):
                halo[section, 2, slot] = zero_half

    def turn_of(at):
        return jnp.where(2 * at < levels, 1, levels - 1)

    turn = turn_of(level)

    def halo_sem(section, k):
        return halo_recv_sem.at[4 if k == 1 else 2 * section + k // 2]

    def halo_copy(section, k, slot, cluster):
        ens = core if slot == 0 else other
        return pltpu.make_async_remote_copy(
            src_ref=halves.at[section, ens],
            dst_ref=halo.at[section, k, slot],
            send_sem=send_sem,
            recv_sem=halo_sem(section, k),
            device_id=(cluster, ens),
            device_id_type=MESH,
        )

    def halo_arrival(section, k):
        return pltpu.make_async_remote_copy(
            src_ref=halo.at[section, k],
            dst_ref=halo.at[section, k],
            send_sem=send_sem,
            recv_sem=halo_sem(section, k),
            device_id=(me, other),
            device_id_type=MESH,
        )

    def coef_sem(section, source, target):
        if section == 0:
            return coef_recv_sem.at[source]
        last = (target + (levels - 1) * turn_of(target)) % levels
        return coef_recv_sem.at[levels + jnp.where(source == last, 1, 0)]

    def coef_copy(section, first, count, cluster):
        return pltpu.make_async_remote_copy(
            src_ref=coef.at[section, pl.ds(first, count)],
            dst_ref=coef.at[section, pl.ds(first, count)],
            send_sem=send_sem,
            recv_sem=coef_sem(section, level, cluster // group),
            device_id=(cluster, core),
            device_id_type=MESH,
        )

    def coef_arrival(section, source, count):
        blocks = coef.at[section, pl.ds(source * group if section == 0 else 0, count)]
        return pltpu.make_async_remote_copy(
            src_ref=blocks,
            dst_ref=blocks,
            send_sem=send_sem,
            recv_sem=coef_sem(section, source, level),
            device_id=(me, other),
            device_id_type=MESH,
        )

    def part_copy(section):
        return pltpu.make_async_remote_copy(
            src_ref=part_send.at[section],
            dst_ref=part_recv.at[section],
            send_sem=send_sem,
            recv_sem=part_recv_sem,
            device_id=(me, other),
            device_id_type=MESH,
        )

    def prepare():
        turned = jnp.transpose(basis_ref[...].astype(jnp.float32)).astype(jnp.bfloat16)
        basis_turned[...] = jnp.concatenate([turned, turned], axis=1)
        loaded(1)
        row = lax.broadcasted_iota(jnp.int32, (widest, group * widest), 0)
        cluster = lax.broadcasted_iota(jnp.int32, (widest, group * widest), 1) // widest
        for source in range(levels):
            block = coupling_ref[:, source * group * widest : (source + 1) * group * widest]
            far = jnp.abs(me - source * group - cluster) > 1
            block = jnp.where(jnp.logical_and(row < own_rank, far), block, 0.0)
            high, low = split(jnp.transpose(block))
            block = jnp.concatenate([high, low], axis=1)
            for j in range(group):
                piece = block[j * widest : (j + 1) * widest]
                far_in[source, 2 * j * widest : (2 * j + 1) * widest] = piece
                far_in[source, (2 * j + 1) * widest : 2 * (j + 1) * widest] = piece
        high, low = split(factors_ref[...])
        far_out[0:widest] = high
        far_out[widest : 2 * widest] = high
        far_out[2 * widest : 3 * widest] = low
        far_out[3 * widest : 4 * widest] = low


    def enter():
        greeted = (
            group * (level + 1)
            + jnp.where(me > 0, 1, 0)
            + jnp.where(me < n - 1, 1, 0)
            + jnp.where(jnp.logical_and(place == group - 1, level < levels - 1), 1, 0)
        )
        pl.semaphore_wait(barrier, greeted)

        def answer(semaphore, cluster):
            pl.semaphore_signal(semaphore, inc=1, device_id=(cluster, core), device_id_type=MESH)

        for d in range(levels - 1, 0, -1):

            @pl.when(level >= d if d > 1 else jnp.logical_and(level > 0, level < levels - 1))
            def _():
                answer(answer_sem, (level - d) * group + place)

        @pl.when(level == levels - 1)
        def _():
            for d in range(group):
                answer(answer_sem, (level - 1) * group + (place + d) % group)

    def rates(section, current_logarithm, early):
        rate = jnp.exp(current_logarithm)
        deficit = (rate - 1.0).astype(jnp.bfloat16)
        halves[section, 0] = deficit[:, :half]
        halves[section, 1] = deficit[:, half:]
        halo[section, 1, 0] = halves[section, core]
        if section == 0:
            basis = basis_ref[...]
            own = lax.dot_general(
                deficit,
                jnp.concatenate([basis, basis], axis=0),
                ROWS,
                preferred_element_type=jnp.float32,
            )
        else:
            own = jnp.dot(deficit, basis_turned[...], preferred_element_type=jnp.float32)
        own = jnp.where(lane_rank < own_rank, own, 0.0)
        high = own.astype(jnp.bfloat16).astype(jnp.float32)
        coef[section, me] = jnp.where(lane < widest, high, own - high).astype(jnp.bfloat16)

        if section == 0:

            @pl.when(me < n - 1)
            def _():
                enter()

            for d in range(group - 1, 0, -1):
                coef_copy(section, me, 1, level * group + (place + d) % group).start()

            for d in range(levels - 1, 0, -1):

                @pl.when(level >= d)
                def _():
                    for p in range(group):
                        coef_copy(section, me, 1, (level - d) * group + p).start()

        else:
            for j in range(n):

                @pl.when(j != me)
                def _():
                    coef_copy(section, me, 1, jnp.int32(j)).start()

        @pl.when(me > 0)
        def _():
            for slot in range(2):
                halo_copy(section, 2, slot, me - 1).start()

        @pl.when(me < n - 1)
        def _():
            for slot in range(2):
                halo_copy(section, 0, slot, me + 1).start()

        halo_copy(section, 1, 1, me).start()

        if section == 0:
            prepare()
            loaded(2)

        def near(k):
            columns = jnp.concatenate([halo[section, k, 0], halo[section, k, 1]], axis=0)
            return lax.dot_general(
                columns, near_ref[k * rows : (k + 1) * rows], ROWS, preferred_element_type=jnp.float32
            )

        if section == 0:
            @pl.when(level == levels - 2)
            def _():
                pl.semaphore_wait(answer_sem, group)
                for d in range(group):
                    coef_copy(section, me, 1, (level + 1) * group + (place + d) % group).start()

            @pl.when(level < levels - 2)
            def _():
                coef_arrival(section, level, group - 1).wait_recv()
                pl.semaphore_wait(answer_sem, levels - 1 - level)
                for d in range(levels - 1, 0, -1):

                    @pl.when(level + d < levels)
                    def _():
                        coef_copy(
                            section, level * group, group, (level + d) * group + place
                        ).start()

        halo_copy(section, 1, 1, me).wait_recv()
        total = near(1)

        @pl.when(me > 0)
        def _():
            halo_arrival(section, 0).wait_recv()

        total = total + near(0)

        @pl.when(me < n - 1)
        def _():
            halo_arrival(section, 2).wait_recv()

        total = total + near(2)
        part_send[section] = total[members:]
        part_copy(section).start()
        early = early(rate)

        if section == 0:

            @pl.when(level >= levels - 2)
            def _():
                coef_arrival(section, level, group - 1).wait_recv()
        else:
            coef_arrival(section, level, n - 1 - group).wait_recv()

        reduced = None
        for d in range(levels):
            source = (level + d * turn) % levels
            if section == 0 and d > 1:
                source = jnp.where(level == levels - 1, d - 2, source)
            if d == levels - 1 or (section == 0 and d > 0):
                coef_arrival(section, source, group).wait_recv()
            coefs = coef[section, pl.ds(source * group, group)]
            coefs = jnp.concatenate([coefs[j] for j in range(group)], axis=1)
            term = jnp.dot(coefs, far_in[source], preferred_element_type=jnp.float32)
            reduced = term if reduced is None else reduced + term
        high, low = split(reduced)
        reduced = jnp.concatenate(
            [jnp.concatenate([high, high], axis=1), jnp.concatenate([low, low], axis=1)], axis=0
        )
        far = jnp.concatenate(
            [
                jnp.dot(reduced, far_out[:, :half], preferred_element_type=jnp.float32),
                jnp.dot(reduced, far_out[:, half:], preferred_element_type=jnp.float32),
            ],
            axis=1,
        )
        stress_rate = total[:members] + (far[:members] + far[members:])
        part_copy(section).wait_recv()
        return stress_rate + part_recv[section], early

    @pl.when(me == n - 1)
    def _():
        enter()

    loaded(0)
    log_rate = log_rate_ref[...]

    def apart(rate, state, state_coef, rate_coef):
        state_rate = jnp.exp(-state) - rate
        return state_rate, state_coef * state_rate, 1.0 / (rate_coef + damping * rate)

    def early_one(rate):
        return apart(rate, friction[0], friction[2], friction[1])

    stress_one, (state_one, healing, inverse) = rates(0, log_rate, early_one)
    rate_one = (stress_one - healing) * inverse

    def early_two(rate):
        return apart(rate, friction[0] + step_length * state_one, friction[2], friction[1])

    stress_two, (state_two, healing, inverse) = rates(
        1, log_rate + step_length * rate_one, early_two
    )
    next_out[0] = log_rate + 0.5 * step_length * (rate_one + (stress_two - healing) * inverse)
    next_out[1] = friction[0] + 0.5 * step_length * (state_one + state_two)

    sent = 2 * (n - 1) * members * 2 * widest * 2 + 2 * (members * half * 2 + members * rows * 4)
    side = 2 * 2 * members * half * 2

    @pl.when(jnp.logical_and(me > 0, me < n - 1))
    def _():
        pltpu.make_async_copy(of_bytes(sent + 2 * side), of_bytes(sent + 2 * side), send_sem).wait()

    @pl.when(jnp.logical_or(me == 0, me == n - 1))
    def _():
        pltpu.make_async_copy(of_bytes(sent + side), of_bytes(sent + side), send_sem).wait()


def finish(next_ref, log_rate_out, state_out, sem):
    copies = [
        pltpu.make_async_copy(next_ref.at[i], target, sem.at[i])
        for i, target in enumerate((log_rate_out, state_out))
    ]
    for copy in copies:
        copy.start()
    for copy in copies:
        copy.wait()


def local(n, *args):
    log_rate, near_weight, col_basis, coupling, factors = (args[i] for i in (0, 4, 5, 6, 7))
    members, rows = log_rate.shape
    half = near_weight.shape[2]
    widest = col_basis.shape[0]
    group = max(d for d in range(1, math.isqrt(n) + 1) if n % d == 0)
    levels = n // group
    f32, bf16 = jnp.float32, jnp.bfloat16
    in_hbm = pl.BlockSpec(memory_space=pltpu.HBM)
    vmem = pl.BlockSpec(memory_space=pltpu.VMEM)
    smem = pl.BlockSpec(memory_space=pltpu.SMEM)
    both = pl.pallas_call(
        functools.partial(kernel, n, group),
        out_shape=pltpu.VMEM((2, members, rows), f32),
        in_specs=[in_hbm] * 8 + [smem],
        out_specs=vmem,
        scratch_shapes=[
            pltpu.VMEM((members, rows), f32),
            pltpu.VMEM(col_basis.shape, bf16),
            pltpu.VMEM((3, members, rows), f32),
            pltpu.VMEM((3 * rows, half), bf16),
            pltpu.VMEM(coupling.shape, f32),
            pltpu.VMEM(factors.shape, f32),
            pltpu.VMEM((rows, 2 * widest), bf16),
            pltpu.VMEM((levels, group * 2 * widest, 2 * widest), bf16),
            pltpu.VMEM((4 * widest, rows), bf16),
            pltpu.VMEM((2, 2, members, half), bf16),
            pltpu.VMEM((2, 3, 2, members, half), bf16),
            pltpu.VMEM((2, n, members, 2 * widest), bf16),
            pltpu.VMEM((2, members, rows), f32),
            pltpu.VMEM((2, members, rows), f32),
            pltpu.SemaphoreType.DMA((3,)),
            pltpu.SemaphoreType.REGULAR,
            pltpu.SemaphoreType.DMA,
            pltpu.SemaphoreType.DMA((5,)),
            pltpu.SemaphoreType.DMA((levels + 2,)),
            pltpu.SemaphoreType.DMA,
        ],
        compiler_params=pltpu.CompilerParams(
            collective_id=0,
            has_side_effects=True,
            vmem_limit_bytes=60 * 1024 * 1024,
        ),
    )(*args[:4], near_weight.reshape(3 * rows, half), *args[5:])
    return tuple(
        pl.pallas_call(
            finish,
            out_shape=[jax.ShapeDtypeStruct((members, rows), f32)] * 2,
            in_specs=[vmem],
            out_specs=[in_hbm] * 2,
            scratch_shapes=[pltpu.SemaphoreType.DMA((2,))],
            compiler_params=pltpu.CompilerParams(vmem_limit_bytes=1024 * 1024),
        )(both)
    )


def solution(mesh):
    in_specs = (
        P("ens", "cluster"),
        P("ens", "cluster"),
        P("ens", "cluster"),
        P("ens", "cluster"),
        P(None, "cluster", "ens"),
        P(None, "cluster"),
        P("cluster", None),
        P(None, "cluster"),
        P("cluster"),
    )
    out_specs = (P("ens", "cluster"), P("ens", "cluster"))
    return jax.shard_map(
        functools.partial(local, mesh.shape["cluster"]),
        mesh=mesh,
        in_specs=in_specs,
        out_specs=out_specs,
        check_vma=False,
    )
```

```python
import functools
import math

import jax
import jax.numpy as jnp
from jax import lax
from jax.experimental import pallas as pl
from jax.experimental.pallas import tpu as pltpu
from jax.sharding import PartitionSpec as P

step_length = 0.5
damping = 0.5

MESH = pl.DeviceIdType.MESH
ROWS = (((1,), (1,)), ((), ()))


def split(value):
    high = value.astype(jnp.bfloat16)
    low = (value - high.astype(jnp.float32)).astype(jnp.bfloat16)
    return high, low


def kernel(
    n,
    group,
    log_rate_hbm,
    state_hbm,
    rate_coef_hbm,
    state_coef_hbm,
    near_hbm,
    basis_hbm,
    coupling_hbm,
    factors_hbm,
    ranks_ref,
    next_out,
    log_rate_ref,
    basis_ref,
    friction,
    near_ref,
    coupling_ref,
    factors_ref,
    basis_turned,
    far_in,
    far_out,
    halves,
    halo,
    coef,
    part_send,
    part_recv,
    load_sem,
    answer_sem,
    send_sem,
    halo_recv_sem,
    coef_recv_sem,
    part_recv_sem,
):
    me = lax.axis_index("cluster")
    core = lax.axis_index("ens")
    other = 1 - core
    levels = n // group
    level = me // group
    place = me % group
    members, rows = log_rate_ref.shape
    half = rows // 2
    widest = basis_ref.shape[0]

    barrier = pltpu.get_barrier_semaphore()

    def greet(cluster, ens):
        pl.semaphore_signal(barrier, inc=1, device_id=(cluster, ens), device_id_type=MESH)

    for d in range(1, group):
        greet(level * group + (place + d) % group, core)
    greet(me, other)

    @pl.when(me > 0)
    def _():
        greet(me - 1, other)

    @pl.when(me < n - 1)
    def _():
        greet(me + 1, other)

    @pl.when(jnp.logical_and(place == 0, level > 0))
    def _():
        greet(me - 1, core)

    for d in range(1, levels):

        @pl.when(level + d < levels)
        def _():
            for p in range(group):
                greet((level + d) * group + p, core)

    def of_bytes(count):
        tiles = count // (16 * 128)
        across = next(c for c in (1, 2, 4) if tiles % c == 0 and 8 * tiles // c <= near_ref.shape[0])
        return near_ref.at[pl.ds(0, 8 * tiles // across), pl.ds(0, 128 * across)]

    loads = (
        (log_rate_hbm, log_rate_ref, 0),
        (basis_hbm, basis_ref, 0),
        (coupling_hbm, coupling_ref, 1),
        (factors_hbm, factors_ref, 1),
        (state_hbm, friction.at[0], 1),
        (rate_coef_hbm, friction.at[1], 1),
        (state_coef_hbm, friction.at[2], 1),
        (near_hbm, near_ref, 2),
    )
    for source, target, i in loads:
        pltpu.make_async_copy(source, target, load_sem.at[i]).start()

    def loaded(i):
        count = sum(math.prod(t.shape) * t.dtype.itemsize for _, t, j in loads if i == j)
        pltpu.make_async_copy(of_bytes(count), of_bytes(count), load_sem.at[i]).wait()

    own_rank = ranks_ref[0]
    lane = lax.broadcasted_iota(jnp.int32, (members, 2 * widest), 1)
    lane_rank = lax.rem(lane, widest)

    zero_half = jnp.zeros((members, half), halo.dtype)
    for section in range(2):

        @pl.when(me == 0)
        def _():
            for slot in range(2):
                halo[section, 0, slot] = zero_half

        @pl.when(me == n - 1)
        def _():
            for slot in range(2):
                halo[section, 2, slot] = zero_half

    def turn_of(at):
        return jnp.where(2 * at < levels, 1, levels - 1)

    turn = turn_of(level)

    def halo_sem(section, k):
        return halo_recv_sem.at[4 if k == 1 else 2 * section + k // 2]

    def halo_copy(section, k, slot, cluster):
        ens = core if slot == 0 else other
        return pltpu.make_async_remote_copy(
            src_ref=halves.at[section, ens],
            dst_ref=halo.at[section, k, slot],
            send_sem=send_sem,
            recv_sem=halo_sem(section, k),
            device_id=(cluster, ens),
            device_id_type=MESH,
        )

    def halo_arrival(section, k):
        return pltpu.make_async_remote_copy(
            src_ref=halo.at[section, k],
            dst_ref=halo.at[section, k],
            send_sem=send_sem,
            recv_sem=halo_sem(section, k),
            device_id=(me, other),
            device_id_type=MESH,
        )

    def coef_sem(section, source, target):
        if section == 0:
            return coef_recv_sem.at[source]
        last = (target + (levels - 1) * turn_of(target)) % levels
        return coef_recv_sem.at[levels + jnp.where(source == last, 1, 0)]

    def coef_copy(section, first, count, cluster):
        return pltpu.make_async_remote_copy(
            src_ref=coef.at[section, pl.ds(first, count)],
            dst_ref=coef.at[section, pl.ds(first, count)],
            send_sem=send_sem,
            recv_sem=coef_sem(section, level, cluster // group),
            device_id=(cluster, core),
            device_id_type=MESH,
        )

    def coef_arrival(section, source, count):
        blocks = coef.at[section, pl.ds(source * group if section == 0 else 0, count)]
        return pltpu.make_async_remote_copy(
            src_ref=blocks,
            dst_ref=blocks,
            send_sem=send_sem,
            recv_sem=coef_sem(section, source, level),
            device_id=(me, other),
            device_id_type=MESH,
        )

    def part_copy(section):
        return pltpu.make_async_remote_copy(
            src_ref=part_send.at[section],
            dst_ref=part_recv.at[section],
            send_sem=send_sem,
            recv_sem=part_recv_sem,
            device_id=(me, other),
            device_id_type=MESH,
        )

    def prepare():
        turned = jnp.transpose(basis_ref[...].astype(jnp.float32)).astype(jnp.bfloat16)
        basis_turned[...] = jnp.concatenate([turned, turned], axis=1)
        loaded(1)
        row = lax.broadcasted_iota(jnp.int32, (widest, group * widest), 0)
        cluster = lax.broadcasted_iota(jnp.int32, (widest, group * widest), 1) // widest
        for source in range(levels):
            block = coupling_ref[:, source * group * widest : (source + 1) * group * widest]
            far = jnp.abs(me - source * group - cluster) > 1
            block = jnp.where(jnp.logical_and(row < own_rank, far), block, 0.0)
            high, low = split(jnp.transpose(block))
            block = jnp.concatenate([high, low], axis=1)
            for j in range(group):
                piece = block[j * widest : (j + 1) * widest]
                far_in[source, 2 * j * widest : (2 * j + 1) * widest] = piece
                far_in[source, (2 * j + 1) * widest : 2 * (j + 1) * widest] = piece
        high, low = split(factors_ref[...])
        far_out[0:widest] = high
        far_out[widest : 2 * widest] = high
        far_out[2 * widest : 3 * widest] = low
        far_out[3 * widest : 4 * widest] = low


    def enter():
        greeted = (
            group * (level + 1)
            + jnp.where(me > 0, 1, 0)
            + jnp.where(me < n - 1, 1, 0)
            + jnp.where(jnp.logical_and(place == group - 1, level < levels - 1), 1, 0)
        )
        pl.semaphore_wait(barrier, greeted)

        def answer(semaphore, cluster):
            pl.semaphore_signal(semaphore, inc=1, device_id=(cluster, core), device_id_type=MESH)

        for d in range(levels - 1, 0, -1):

            @pl.when(level >= d if d > 1 else jnp.logical_and(level > 0, level < levels - 1))
            def _():
                answer(answer_sem, (level - d) * group + place)

        @pl.when(level == levels - 1)
        def _():
            for d in range(group):
                answer(answer_sem, (level - 1) * group + (place + d) % group)

    def rates(section, current_logarithm, early):
        rate = jnp.exp(current_logarithm)
        deficit = (rate - 1.0).astype(jnp.bfloat16)
        halves[section, 0] = deficit[:, :half]
        halves[section, 1] = deficit[:, half:]
        halo[section, 1, 0] = halves[section, core]
        if section == 0:
            basis = basis_ref[...]
            own = lax.dot_general(
                deficit,
                jnp.concatenate([basis, basis], axis=0),
                ROWS,
                preferred_element_type=jnp.float32,
            )
        else:
            own = jnp.dot(deficit, basis_turned[...], preferred_element_type=jnp.float32)
        own = jnp.where(lane_rank < own_rank, own, 0.0)
        high = own.astype(jnp.bfloat16).astype(jnp.float32)
        coef[section, me] = jnp.where(lane < widest, high, own - high).astype(jnp.bfloat16)

        if section == 0:

            @pl.when(me < n - 1)
            def _():
                enter()

            for d in range(group - 1, 0, -1):
                coef_copy(section, me, 1, level * group + (place + d) % group).start()

            for d in range(levels - 1, 0, -1):

                @pl.when(level >= d)
                def _():
                    for p in range(group):
                        coef_copy(section, me, 1, (level - d) * group + p).start()

        else:
            for j in range(n):

                @pl.when(j != me)
                def _():
                    coef_copy(section, me, 1, jnp.int32(j)).start()

        @pl.when(me > 0)
        def _():
            for slot in range(2):
                halo_copy(section, 2, slot, me - 1).start()

        @pl.when(me < n - 1)
        def _():
            for slot in range(2):
                halo_copy(section, 0, slot, me + 1).start()

        halo_copy(section, 1, 1, me).start()

        if section == 0:
            prepare()
            loaded(2)

        def near(k):
            columns = jnp.concatenate([halo[section, k, 0], halo[section, k, 1]], axis=0)
            return lax.dot_general(
                columns, near_ref[k * rows : (k + 1) * rows], ROWS, preferred_element_type=jnp.float32
            )

        if section == 0:
            @pl.when(level == levels - 2)
            def _():
                pl.semaphore_wait(answer_sem, group)
                for d in range(group):
                    coef_copy(section, me, 1, (level + 1) * group + (place + d) % group).start()

            @pl.when(level < levels - 2)
            def _():
                coef_arrival(section, level, group - 1).wait_recv()
                pl.semaphore_wait(answer_sem, levels - 1 - level)
                for d in range(levels - 1, 0, -1):

                    @pl.when(level + d < levels)
                    def _():
                        coef_copy(
                            section, level * group, group, (level + d) * group + place
                        ).start()

        halo_copy(section, 1, 1, me).wait_recv()
        total = near(1)

        @pl.when(me > 0)
        def _():
            halo_arrival(section, 0).wait_recv()

        total = total + near(0)

        @pl.when(me < n - 1)
        def _():
            halo_arrival(section, 2).wait_recv()

        total = total + near(2)
        part_send[section] = total[members:]
        part_copy(section).start()
        early = early(rate)

        if section == 0:

            @pl.when(level >= levels - 2)
            def _():
                coef_arrival(section, level, group - 1).wait_recv()
        else:
            coef_arrival(section, level, n - 1 - group).wait_recv()

        reduced = None
        for d in range(levels):
            source = (level + d * turn) % levels
            if section == 0 and d > 1:
                source = jnp.where(level == levels - 1, d - 2, source)
            if d == levels - 1 or (section == 0 and d > 0):
                coef_arrival(section, source, group).wait_recv()
            coefs = coef[section, pl.ds(source * group, group)]
            coefs = jnp.concatenate([coefs[j] for j in range(group)], axis=1)
            term = jnp.dot(coefs, far_in[source], preferred_element_type=jnp.float32)
            reduced = term if reduced is None else reduced + term
        high, low = split(reduced)
        reduced = jnp.concatenate(
            [jnp.concatenate([high, high], axis=1), jnp.concatenate([low, low], axis=1)], axis=0
        )
        far = jnp.concatenate(
            [
                jnp.dot(reduced, far_out[:, :half], preferred_element_type=jnp.float32),
                jnp.dot(reduced, far_out[:, half:], preferred_element_type=jnp.float32),
            ],
            axis=1,
        )
        stress_rate = total[:members] + (far[:members] + far[members:])
        part_copy(section).wait_recv()
        return stress_rate + part_recv[section], early

    @pl.when(me == n - 1)
    def _():
        enter()

    loaded(0)
    log_rate = log_rate_ref[...]

    def apart(rate, state, state_coef, rate_coef):
        state_rate = jnp.exp(-state) - rate
        return state_rate, state_coef * state_rate, 1.0 / (rate_coef + damping * rate)

    def early_one(rate):
        return apart(rate, friction[0], friction[2], friction[1])

    stress_one, (state_one, healing, inverse) = rates(0, log_rate, early_one)
    rate_one = (stress_one - healing) * inverse

    def early_two(rate):
        state_two, healing, inverse = apart(
            rate, friction[0] + step_length * state_one, friction[2], friction[1]
        )
        next_out[1] = friction[0] + 0.5 * step_length * (state_one + state_two)
        gain = 0.5 * step_length * inverse
        return log_rate + 0.5 * step_length * rate_one - gain * healing, gain

    stress_two, (settled, gain) = rates(
        1, log_rate + step_length * rate_one, early_two
    )
    next_out[0] = settled + gain * stress_two

    sent = 2 * (n - 1) * members * 2 * widest * 2 + 2 * (members * half * 2 + members * rows * 4)
    side = 2 * 2 * members * half * 2

    @pl.when(jnp.logical_and(me > 0, me < n - 1))
    def _():
        pltpu.make_async_copy(of_bytes(sent + 2 * side), of_bytes(sent + 2 * side), send_sem).wait()

    @pl.when(jnp.logical_or(me == 0, me == n - 1))
    def _():
        pltpu.make_async_copy(of_bytes(sent + side), of_bytes(sent + side), send_sem).wait()


def finish(next_ref, log_rate_out, state_out, sem):
    copies = [
        pltpu.make_async_copy(next_ref.at[i], target, sem.at[i])
        for i, target in enumerate((log_rate_out, state_out))
    ]
    for copy in copies:
        copy.start()
    for copy in copies:
        copy.wait()


def local(n, *args):
    log_rate, near_weight, col_basis, coupling, factors = (args[i] for i in (0, 4, 5, 6, 7))
    members, rows = log_rate.shape
    half = near_weight.shape[2]
    widest = col_basis.shape[0]
    group = max(d for d in range(1, math.isqrt(n) + 1) if n % d == 0)
    levels = n // group
    f32, bf16 = jnp.float32, jnp.bfloat16
    in_hbm = pl.BlockSpec(memory_space=pltpu.HBM)
    vmem = pl.BlockSpec(memory_space=pltpu.VMEM)
    smem = pl.BlockSpec(memory_space=pltpu.SMEM)
    both = pl.pallas_call(
        functools.partial(kernel, n, group),
        out_shape=pltpu.VMEM((2, members, rows), f32),
        in_specs=[in_hbm] * 8 + [smem],
        out_specs=vmem,
        scratch_shapes=[
            pltpu.VMEM((members, rows), f32),
            pltpu.VMEM(col_basis.shape, bf16),
            pltpu.VMEM((3, members, rows), f32),
            pltpu.VMEM((3 * rows, half), bf16),
            pltpu.VMEM(coupling.shape, f32),
            pltpu.VMEM(factors.shape, f32),
            pltpu.VMEM((rows, 2 * widest), bf16),
            pltpu.VMEM((levels, group * 2 * widest, 2 * widest), bf16),
            pltpu.VMEM((4 * widest, rows), bf16),
            pltpu.VMEM((2, 2, members, half), bf16),
            pltpu.VMEM((2, 3, 2, members, half), bf16),
            pltpu.VMEM((2, n, members, 2 * widest), bf16),
            pltpu.VMEM((2, members, rows), f32),
            pltpu.VMEM((2, members, rows), f32),
            pltpu.SemaphoreType.DMA((3,)),
            pltpu.SemaphoreType.REGULAR,
            pltpu.SemaphoreType.DMA,
            pltpu.SemaphoreType.DMA((5,)),
            pltpu.SemaphoreType.DMA((levels + 2,)),
            pltpu.SemaphoreType.DMA,
        ],
        compiler_params=pltpu.CompilerParams(
            collective_id=0,
            has_side_effects=True,
            vmem_limit_bytes=60 * 1024 * 1024,
        ),
    )(*args[:4], near_weight.reshape(3 * rows, half), *args[5:])
    return tuple(
        pl.pallas_call(
            finish,
            out_shape=[jax.ShapeDtypeStruct((members, rows), f32)] * 2,
            in_specs=[vmem],
            out_specs=[in_hbm] * 2,
            scratch_shapes=[pltpu.SemaphoreType.DMA((2,))],
            compiler_params=pltpu.CompilerParams(vmem_limit_bytes=1024 * 1024),
        )(both)
    )


def solution(mesh):
    in_specs = (
        P("ens", "cluster"),
        P("ens", "cluster"),
        P("ens", "cluster"),
        P("ens", "cluster"),
        P(None, "cluster", "ens"),
        P(None, "cluster"),
        P("cluster", None),
        P(None, "cluster"),
        P("cluster"),
    )
    out_specs = (P("ens", "cluster"), P("ens", "cluster"))
    return jax.shard_map(
        functools.partial(local, mesh.shape["cluster"]),
        mesh=mesh,
        in_specs=in_specs,
        out_specs=out_specs,
        check_vma=False,
    )
```

```python
import functools
import math

import jax
import jax.numpy as jnp
from jax import lax
from jax.experimental import pallas as pl
from jax.experimental.pallas import tpu as pltpu
from jax.sharding import PartitionSpec as P

step_length = 0.5
damping = 0.5

MESH = pl.DeviceIdType.MESH
ROWS = (((1,), (1,)), ((), ()))


def split(value):
    high = value.astype(jnp.bfloat16)
    low = (value - high.astype(jnp.float32)).astype(jnp.bfloat16)
    return high, low


def kernel(
    n,
    group,
    log_rate_hbm,
    state_hbm,
    rate_coef_hbm,
    state_coef_hbm,
    near_hbm,
    basis_hbm,
    coupling_hbm,
    factors_hbm,
    ranks_ref,
    next_out,
    log_rate_ref,
    basis_ref,
    friction,
    near_ref,
    coupling_ref,
    factors_ref,
    basis_turned,
    far_in,
    far_out,
    halves,
    halo,
    coef,
    part_send,
    part_recv,
    load_sem,
    answer_sem,
    send_sem,
    halo_recv_sem,
    coef_recv_sem,
    part_recv_sem,
):
    me = lax.axis_index("cluster")
    core = lax.axis_index("ens")
    other = 1 - core
    levels = n // group
    level = me // group
    place = me % group
    members, rows = log_rate_ref.shape
    half = rows // 2
    widest = basis_ref.shape[0]

    barrier = pltpu.get_barrier_semaphore()

    def greet(cluster, ens):
        pl.semaphore_signal(barrier, inc=1, device_id=(cluster, ens), device_id_type=MESH)

    for d in range(1, group):
        greet(level * group + (place + d) % group, core)
    greet(me, other)

    @pl.when(me > 0)
    def _():
        greet(me - 1, other)

    @pl.when(me < n - 1)
    def _():
        greet(me + 1, other)

    @pl.when(jnp.logical_and(place == 0, level > 0))
    def _():
        greet(me - 1, core)

    for d in range(1, levels):

        @pl.when(level + d < levels)
        def _():
            for p in range(group):
                greet((level + d) * group + p, core)

    def of_bytes(count):
        tiles = count // (16 * 128)
        across = next(c for c in (1, 2, 4) if tiles % c == 0 and 8 * tiles // c <= near_ref.shape[0])
        return near_ref.at[pl.ds(0, 8 * tiles // across), pl.ds(0, 128 * across)]

    loads = (
        (log_rate_hbm, log_rate_ref, 0),
        (basis_hbm, basis_ref, 0),
        (coupling_hbm, coupling_ref, 1),
        (factors_hbm, factors_ref, 1),
        (state_hbm, friction.at[0], 1),
        (rate_coef_hbm, friction.at[1], 1),
        (state_coef_hbm, friction.at[2], 1),
        (near_hbm, near_ref, 2),
    )
    for source, target, i in loads:
        pltpu.make_async_copy(source, target, load_sem.at[i]).start()

    def loaded(i):
        count = sum(math.prod(t.shape) * t.dtype.itemsize for _, t, j in loads if i == j)
        pltpu.make_async_copy(of_bytes(count), of_bytes(count), load_sem.at[i]).wait()

    own_rank = ranks_ref[0]
    lane = lax.broadcasted_iota(jnp.int32, (members, 2 * widest), 1)
    lane_rank = lax.rem(lane, widest)

    zero_half = jnp.zeros((members, half), halo.dtype)
    for section in range(2):

        @pl.when(me == 0)
        def _():
            for slot in range(2):
                halo[section, 0, slot] = zero_half

        @pl.when(me == n - 1)
        def _():
            for slot in range(2):
                halo[section, 2, slot] = zero_half

    def turn_of(at):
        return jnp.where(2 * at < levels, 1, levels - 1)

    turn = turn_of(level)

    def halo_sem(section, k):
        return halo_recv_sem.at[4 if k == 1 else 2 * section + k // 2]

    def halo_copy(section, k, slot, cluster):
        ens = core if slot == 0 else other
        return pltpu.make_async_remote_copy(
            src_ref=halves.at[section, ens],
            dst_ref=halo.at[section, k, slot],
            send_sem=send_sem,
            recv_sem=halo_sem(section, k),
            device_id=(cluster, ens),
            device_id_type=MESH,
        )

    def halo_arrival(section, k):
        return pltpu.make_async_remote_copy(
            src_ref=halo.at[section, k],
            dst_ref=halo.at[section, k],
            send_sem=send_sem,
            recv_sem=halo_sem(section, k),
            device_id=(me, other),
            device_id_type=MESH,
        )

    def coef_sem(section, source, target):
        if section == 0:
            return coef_recv_sem.at[source]
        last = (target + (levels - 1) * turn_of(target)) % levels
        return coef_recv_sem.at[levels + jnp.where(source == last, 1, 0)]

    def coef_copy(section, first, count, cluster):
        return pltpu.make_async_remote_copy(
            src_ref=coef.at[section, pl.ds(first, count)],
            dst_ref=coef.at[section, pl.ds(first, count)],
            send_sem=send_sem,
            recv_sem=coef_sem(section, level, cluster // group),
            device_id=(cluster, core),
            device_id_type=MESH,
        )

    def coef_arrival(section, source, count):
        blocks = coef.at[section, pl.ds(source * group if section == 0 else 0, count)]
        return pltpu.make_async_remote_copy(
            src_ref=blocks,
            dst_ref=blocks,
            send_sem=send_sem,
            recv_sem=coef_sem(section, source, level),
            device_id=(me, other),
            device_id_type=MESH,
        )

    def part_copy(section):
        return pltpu.make_async_remote_copy(
            src_ref=part_send.at[section],
            dst_ref=part_recv.at[section],
            send_sem=send_sem,
            recv_sem=part_recv_sem,
            device_id=(me, other),
            device_id_type=MESH,
        )

    def prepare():
        turned = jnp.transpose(basis_ref[...].astype(jnp.float32)).astype(jnp.bfloat16)
        basis_turned[...] = jnp.concatenate([turned, turned], axis=1)
        loaded(1)
        row = lax.broadcasted_iota(jnp.int32, (widest, group * widest), 0)
        cluster = lax.broadcasted_iota(jnp.int32, (widest, group * widest), 1) // widest
        for source in range(levels):
            block = coupling_ref[:, source * group * widest : (source + 1) * group * widest]
            far = jnp.abs(me - source * group - cluster) > 1
            block = jnp.where(jnp.logical_and(row < own_rank, far), block, 0.0)
            high, low = split(jnp.transpose(block))
            block = jnp.concatenate([high, low], axis=1)
            for j in range(group):
                piece = block[j * widest : (j + 1) * widest]
                far_in[source, 2 * j * widest : (2 * j + 1) * widest] = piece
                far_in[source, (2 * j + 1) * widest : 2 * (j + 1) * widest] = piece
        high, low = split(factors_ref[...])
        far_out[0:widest] = high
        far_out[widest : 2 * widest] = high
        far_out[2 * widest : 3 * widest] = low
        far_out[3 * widest : 4 * widest] = low


    def enter():
        greeted = (
            group * (level + 1)
            + jnp.where(me > 0, 1, 0)
            + jnp.where(me < n - 1, 1, 0)
            + jnp.where(jnp.logical_and(place == group - 1, level < levels - 1), 1, 0)
        )
        pl.semaphore_wait(barrier, greeted)

        def answer(semaphore, cluster):
            pl.semaphore_signal(semaphore, inc=1, device_id=(cluster, core), device_id_type=MESH)

        for d in range(levels - 1, 0, -1):

            @pl.when(level >= d if d > 1 else jnp.logical_and(level > 0, level < levels - 1))
            def _():
                answer(answer_sem, (level - d) * group + place)

        @pl.when(level == levels - 1)
        def _():
            for d in range(group):
                answer(answer_sem, (level - 1) * group + (place + d) % group)

    def rates(section, current_logarithm, early):
        rate = jnp.exp(current_logarithm)
        deficit = (rate - 1.0).astype(jnp.bfloat16)
        halves[section, 0] = deficit[:, :half]
        halves[section, 1] = deficit[:, half:]
        halo[section, 1, 0] = halves[section, core]
        if section == 0:
            basis = basis_ref[...]
            own = lax.dot_general(
                deficit,
                jnp.concatenate([basis, basis], axis=0),
                ROWS,
                preferred_element_type=jnp.float32,
            )
        else:
            own = jnp.dot(deficit, basis_turned[...], preferred_element_type=jnp.float32)
        own = jnp.where(lane_rank < own_rank, own, 0.0)
        high = own.astype(jnp.bfloat16).astype(jnp.float32)
        coef[section, me] = jnp.where(lane < widest, high, own - high).astype(jnp.bfloat16)

        if section == 0:

            @pl.when(me < n - 1)
            def _():
                enter()

            for d in range(group - 1, 0, -1):
                coef_copy(section, me, 1, level * group + (place + d) % group).start()

            for d in range(levels - 1, 0, -1):

                @pl.when(level >= d)
                def _():
                    for p in range(group):
                        coef_copy(section, me, 1, (level - d) * group + p).start()

        else:
            for j in range(n):

                @pl.when(j != me)
                def _():
                    coef_copy(section, me, 1, jnp.int32(j)).start()

        @pl.when(me > 0)
        def _():
            for slot in range(2):
                halo_copy(section, 2, slot, me - 1).start()

        @pl.when(me < n - 1)
        def _():
            for slot in range(2):
                halo_copy(section, 0, slot, me + 1).start()

        halo_copy(section, 1, 1, me).start()

        if section == 0:
            prepare()
            loaded(2)

        def near(k):
            columns = jnp.concatenate([halo[section, k, 0], halo[section, k, 1]], axis=0)
            return lax.dot_general(
                columns, near_ref[k * rows : (k + 1) * rows], ROWS, preferred_element_type=jnp.float32
            )

        if section == 0:
            @pl.when(level == levels - 2)
            def _():
                pl.semaphore_wait(answer_sem, group)
                for d in range(group):
                    coef_copy(section, me, 1, (level + 1) * group + (place + d) % group).start()

            @pl.when(level < levels - 2)
            def _():
                coef_arrival(section, level, group - 1).wait_recv()
                pl.semaphore_wait(answer_sem, levels - 1 - level)
                for d in range(levels - 1, 0, -1):

                    @pl.when(level + d < levels)
                    def _():
                        coef_copy(
                            section, level * group, group, (level + d) * group + place
                        ).start()

        halo_copy(section, 1, 1, me).wait_recv()
        total = near(1)

        @pl.when(me > 0)
        def _():
            halo_arrival(section, 0).wait_recv()

        total = total + near(0)

        @pl.when(me < n - 1)
        def _():
            halo_arrival(section, 2).wait_recv()

        total = total + near(2)
        part_send[section] = total[members:]
        part_copy(section).start()
        early = early(rate)

        if section == 0:

            @pl.when(level >= levels - 2)
            def _():
                coef_arrival(section, level, group - 1).wait_recv()
        else:
            coef_arrival(section, level, n - 1 - group).wait_recv()

        reduced = None
        for d in range(levels):
            source = (level + d * turn) % levels
            if section == 0 and d > 1:
                source = jnp.where(level == levels - 1, d - 2, source)
            if d == levels - 1 or (section == 0 and d > 0):
                coef_arrival(section, source, group).wait_recv()
            coefs = coef[section, pl.ds(source * group, group)]
            coefs = jnp.concatenate([coefs[j] for j in range(group)], axis=1)
            term = jnp.dot(coefs, far_in[source], preferred_element_type=jnp.float32)
            reduced = term if reduced is None else reduced + term
        high, low = split(reduced)
        reduced = jnp.concatenate(
            [jnp.concatenate([high, high], axis=1), jnp.concatenate([low, low], axis=1)], axis=0
        )
        far = jnp.concatenate(
            [
                jnp.dot(reduced, far_out[:, :half], preferred_element_type=jnp.float32),
                jnp.dot(reduced, far_out[:, half:], preferred_element_type=jnp.float32),
            ],
            axis=1,
        )
        stress_rate = total[:members] + (far[:members] + far[members:])
        part_copy(section).wait_recv()
        return stress_rate + part_recv[section], early

    @pl.when(me == n - 1)
    def _():
        enter()

    loaded(0)
    log_rate = log_rate_ref[...]

    def apart(rate, state, state_coef, rate_coef):
        state_rate = jnp.exp(-state) - rate
        return state_rate, state_coef * state_rate, 1.0 / (rate_coef + damping * rate)

    def early_one(rate):
        state_one, healing, inverse = apart(rate, friction[0], friction[2], friction[1])
        gain = step_length * inverse
        return state_one, healing, inverse, log_rate - gain * healing, gain

    stress_one, (state_one, healing, inverse, still, gain) = rates(0, log_rate, early_one)
    rate_one = (stress_one - healing) * inverse

    def early_two(rate):
        state_two, healing, inverse = apart(
            rate, friction[0] + step_length * state_one, friction[2], friction[1]
        )
        next_out[1] = friction[0] + 0.5 * step_length * (state_one + state_two)
        gain = 0.5 * step_length * inverse
        return log_rate + 0.5 * step_length * rate_one - gain * healing, gain

    stress_two, (settled, gain) = rates(
        1, still + gain * stress_one, early_two
    )
    next_out[0] = settled + gain * stress_two

    sent = 2 * (n - 1) * members * 2 * widest * 2 + 2 * (members * half * 2 + members * rows * 4)
    side = 2 * 2 * members * half * 2

    @pl.when(jnp.logical_and(me > 0, me < n - 1))
    def _():
        pltpu.make_async_copy(of_bytes(sent + 2 * side), of_bytes(sent + 2 * side), send_sem).wait()

    @pl.when(jnp.logical_or(me == 0, me == n - 1))
    def _():
        pltpu.make_async_copy(of_bytes(sent + side), of_bytes(sent + side), send_sem).wait()


def finish(next_ref, log_rate_out, state_out, sem):
    copies = [
        pltpu.make_async_copy(next_ref.at[i], target, sem.at[i])
        for i, target in enumerate((log_rate_out, state_out))
    ]
    for copy in copies:
        copy.start()
    for copy in copies:
        copy.wait()


def local(n, *args):
    log_rate, near_weight, col_basis, coupling, factors = (args[i] for i in (0, 4, 5, 6, 7))
    members, rows = log_rate.shape
    half = near_weight.shape[2]
    widest = col_basis.shape[0]
    group = max(d for d in range(1, math.isqrt(n) + 1) if n % d == 0)
    levels = n // group
    f32, bf16 = jnp.float32, jnp.bfloat16
    in_hbm = pl.BlockSpec(memory_space=pltpu.HBM)
    vmem = pl.BlockSpec(memory_space=pltpu.VMEM)
    smem = pl.BlockSpec(memory_space=pltpu.SMEM)
    both = pl.pallas_call(
        functools.partial(kernel, n, group),
        out_shape=pltpu.VMEM((2, members, rows), f32),
        in_specs=[in_hbm] * 8 + [smem],
        out_specs=vmem,
        scratch_shapes=[
            pltpu.VMEM((members, rows), f32),
            pltpu.VMEM(col_basis.shape, bf16),
            pltpu.VMEM((3, members, rows), f32),
            pltpu.VMEM((3 * rows, half), bf16),
            pltpu.VMEM(coupling.shape, f32),
            pltpu.VMEM(factors.shape, f32),
            pltpu.VMEM((rows, 2 * widest), bf16),
            pltpu.VMEM((levels, group * 2 * widest, 2 * widest), bf16),
            pltpu.VMEM((4 * widest, rows), bf16),
            pltpu.VMEM((2, 2, members, half), bf16),
            pltpu.VMEM((2, 3, 2, members, half), bf16),
            pltpu.VMEM((2, n, members, 2 * widest), bf16),
            pltpu.VMEM((2, members, rows), f32),
            pltpu.VMEM((2, members, rows), f32),
            pltpu.SemaphoreType.DMA((3,)),
            pltpu.SemaphoreType.REGULAR,
            pltpu.SemaphoreType.DMA,
            pltpu.SemaphoreType.DMA((5,)),
            pltpu.SemaphoreType.DMA((levels + 2,)),
            pltpu.SemaphoreType.DMA,
        ],
        compiler_params=pltpu.CompilerParams(
            collective_id=0,
            has_side_effects=True,
            vmem_limit_bytes=60 * 1024 * 1024,
        ),
    )(*args[:4], near_weight.reshape(3 * rows, half), *args[5:])
    return tuple(
        pl.pallas_call(
            finish,
            out_shape=[jax.ShapeDtypeStruct((members, rows), f32)] * 2,
            in_specs=[vmem],
            out_specs=[in_hbm] * 2,
            scratch_shapes=[pltpu.SemaphoreType.DMA((2,))],
            compiler_params=pltpu.CompilerParams(vmem_limit_bytes=1024 * 1024),
        )(both)
    )


def solution(mesh):
    in_specs = (
        P("ens", "cluster"),
        P("ens", "cluster"),
        P("ens", "cluster"),
        P("ens", "cluster"),
        P(None, "cluster", "ens"),
        P(None, "cluster"),
        P("cluster", None),
        P(None, "cluster"),
        P("cluster"),
    )
    out_specs = (P("ens", "cluster"), P("ens", "cluster"))
    return jax.shard_map(
        functools.partial(local, mesh.shape["cluster"]),
        mesh=mesh,
        in_specs=in_specs,
        out_specs=out_specs,
        check_vma=False,
    )
```
